32 devices in a mesh: sub: 8 (over y, x, core), rep: 4 (over z).
Axes of the slice: x: 2, y: 2, z: 4, core: 2. Of those that a mesh axis runs over, the one named last changes fastest.
Arguments:
- loads: bfloat16 [64, 256, 1024], P('sub', 'rep'), may hold values from -6 to 6
- operators: bfloat16 [64, 1024, 1024], P('sub'), may hold values from -0.1875 to 0.1875
- owner: int32 [512, 1], P('sub'), may hold values from 0 to 7; in each aligned block of 64 rows (0 to 63, 64 to 127, ...) at most 16 rows name the same one
- dual_block: int32 [512], P('sub'), may hold values from 0 to 15
- scale_index: int32 [16384], P('sub'), may hold values from 0 to 3
- basis: bfloat16 [16384, 1024], P('sub'), may hold values from -0.046875 to 0.046875
- coarse: bfloat16 [1024, 1024], replicated, may hold values from -0.75 to 0.75
Outputs:
- start: float32 [256, 16384], P('rep', 'sub')
- resid: float32 [256, 16384], P('rep', 'sub')
The draws below stay inside these ranges and needn't reach their ends.
Inputs may be any that keep to these rules, and one draw needn't show every extreme that they name: Among the blocks of the subdomains of one index of sub (aligned blocks of 64 rows), no owner is named more than 16 times, a bound that some block reaches.
All inputs are finite; a program needn't handle non-finite values.
Results may differ from the reference program's by a relative error of at most 0.0075.
Values may be sent and summed in bfloat16 or wider, within the bound.
A program may use at most 128 MiB of HBM per device.

```python
import math
import jax
import jax.numpy as jnp
import numpy as np
from jax import lax

L = 1024
BLK = 128
NB = 1024
K = 256
SUB_DEV = 8
OB = 16
BPS = 8
CAP = 16
SUBS = 64
NDUAL = 16384
N_SUB = 8


def plant(values, rng, smallest, top_value):
    place = [jax.random.randint(jax.random.fold_in(rng, axis), (), 0, length) for axis, length in enumerate(values.shape)]
    widest = values.shape.index(max(values.shape))
    beside = place[:widest] + [(place[widest] + 1) % values.shape[widest]] + place[widest + 1:]
    return values.at[tuple(place)].set(smallest).at[tuple(beside)].set(top_value)


def level_of(own_key, extent, shards, smallest, largest):
    factor_of = 1.0
    for axis_at, parts in shards:
        heights = jax.random.uniform(jax.random.fold_in(jax.random.fold_in(own_key, 6), axis_at), (parts,), jnp.float32, smallest / len(shards), largest / len(shards))
        factor_of = factor_of * jnp.repeat(jnp.exp(heights), extent[axis_at] // parts).reshape((-1,) + (1,) * (len(extent) - 1 - axis_at))
    return factor_of


def deal_out(key, own, number, rows, count, top, limit, skew):
    sequence = jax.random.permutation(key, count)
    packed, ordinary = load_shares(count, rows * top, limit, skew, True), load_shares(count, rows * top, limit, skew, False)
    places = jnp.arange(count)

    def named(lengths, rotation):
        used = int((lengths > 0).sum())
        fixed = max(1, used // 4)
        moved = fixed + (places - fixed + rotation * (used - fixed)) % max(1, count - fixed)
        return jnp.zeros((count,), jnp.int32).at[sequence[jnp.where(places < fixed, places, moved)]].set(jnp.asarray(lengths, jnp.int32))

    lengths = jnp.where(number % 4 == 0, named(packed, number // 4), named(ordinary, number - number // 4 - 1))
    mixed = jax.random.permutation(jax.random.fold_in(own, 3), count)
    donor, receiver = mixed[0:count // 2 * 2:2], mixed[1:count // 2 * 2:2]
    margin = jnp.minimum(lengths[donor] - 1, limit - lengths[receiver]) // 2
    margin = jnp.where((donor == sequence[0]) | (receiver == sequence[0]) | (lengths[receiver] == 0), 0, jnp.maximum(margin, 0))
    moved = jax.random.randint(jax.random.fold_in(own, 4), (count // 2,), 0, 1 << 20) % (margin + 1)
    lengths = lengths.at[donor].add(-moved).at[receiver].add(moved)
    items = jnp.searchsorted(jnp.cumsum(lengths), jnp.arange(rows * top), side="right").astype(jnp.int32)
    grid = items.reshape(top, rows).T
    grid = grid[jax.random.permutation(jax.random.fold_in(own, 1), rows)]
    rotation = jax.random.randint(jax.random.fold_in(own, 2), (rows, 1), 0, top)
    return jnp.take_along_axis(grid, (jnp.arange(top)[None, :] + rotation) % top, axis=1)


def load_shares(number_of, total, bound, skew, full):
    weights = [(1 << 20) // math.isqrt(grade ** skew) + 1 for grade in range(1, number_of + 1)]
    largest = bound if full else min(bound, max(-(-total // number_of), total * weights[0] // sum(weights)))
    least = 1 if total - largest >= number_of - 1 else 0
    counts, spare = [largest] + [least] * (number_of - 1), total - largest - least * (number_of - 1)
    while spare > 0:
        candidates = [i for i in range(1, number_of) if counts[i] < largest] or [i for i in range(1, number_of) if counts[i] < bound]
        pool, budget = sum([weights[i] for i in candidates]), spare
        for i in candidates:
            addition = min(bound - counts[i], max(1, budget * weights[i] // pool), spare)
            counts[i] = counts[i] + addition
            spare = spare - addition
    return np.array(counts)


def gaussian(stream_key, extent, deviation, limit, shards=(), kind=jnp.bfloat16):
    result = deviation * jax.random.normal(stream_key, extent, jnp.float32)
    if shards:
        result = result * level_of(stream_key, extent, shards, -0.22, 0.18)
    return jnp.clip(result, -limit, limit).astype(kind)


def setup_inputs(seed: int = 0) -> dict:
    key_of = jax.random.split(jax.random.key(seed), 8)
    loads = gaussian(key_of[0], (SUBS, K, L), 1.0, 6.0, ((0, 8), (1, 4)))
    operators = gaussian(key_of[1], (SUBS, L, L), L ** -0.5, 0.1875, ((0, 8),))
    owner_keys = jax.random.split(jax.random.fold_in(key_of[2], 1), (SUBS * BPS) // (SUB_DEV * BPS))
    owner_turns = jax.random.permutation(jax.random.fold_in(key_of[2], 3), (SUBS * BPS) // (SUB_DEV * BPS))
    owner = jax.vmap(lambda own, number: deal_out(jax.random.fold_in(key_of[2], 2), own, number, SUB_DEV * BPS, N_SUB, 1, CAP, 2))(owner_keys, owner_turns).reshape((SUBS * BPS, 1))
    dual_block = plant(jax.random.randint(key_of[3], (SUBS * BPS,), 0, OB), jax.random.fold_in(key_of[3], 1), 0, OB - 1).astype(jnp.int32)
    scale_index = plant(jax.random.randint(key_of[4], (NDUAL,), 0, 4), jax.random.fold_in(key_of[4], 1), 0, 3).astype(jnp.int32)
    basis = gaussian(key_of[5], (NDUAL, NB), NDUAL ** -0.5, 0.046875, ((0, 8),))
    coarse = gaussian(key_of[6], (NB, NB), (max(1, NB * NB // NDUAL)) ** -0.5, 0.75)
    return {"loads": loads, "operators": operators, "owner": owner, "dual_block": dual_block, "scale_index": scale_index, "basis": basis, "coarse": coarse}


def apply_all(inputs, operators):
    def one(pair):
        return jnp.dot(pair[0], pair[1], preferred_element_type=jnp.float32).astype(jnp.bfloat16)
    return lax.map(one, (inputs, operators))


def to_blocks(values):
    return values.reshape(SUBS, K, BPS, BLK).transpose(0, 2, 1, 3).reshape(SUBS * BPS, K, BLK)


def collect(values, targets, weight):
    blocks = to_blocks(values).astype(jnp.float32)
    total = jnp.zeros((NDUAL // BLK, K, BLK), jnp.float32).at[targets].add(blocks)
    return total.transpose(1, 0, 2).reshape(K, NDUAL) * weight[None, :]


def reference(loads, operators, owner, dual_block, scale_index, basis, coarse):
    targets = (owner[:, 0] * OB + dual_block).astype(jnp.int32)
    weight = 1.0 / (1.0 + scale_index.astype(jnp.float32))
    terms = apply_all(loads, operators)
    dual = collect(terms, targets, weight)
    coeff = jnp.dot(dual.astype(jnp.bfloat16), basis, preferred_element_type=jnp.float32)
    solved = jnp.dot(coeff.astype(jnp.bfloat16), coarse, preferred_element_type=jnp.float32).astype(jnp.bfloat16)
    start = lax.dot_general(solved, basis, (((1,), (1,)), ((), ())), preferred_element_type=jnp.float32)
    start_blocks = start.astype(jnp.bfloat16).reshape(K, NDUAL // BLK, BLK).transpose(1, 0, 2)
    picked = start_blocks[targets]
    local = picked.reshape(SUBS, BPS, K, BLK).transpose(0, 2, 1, 3).reshape(SUBS, K, L)
    again = apply_all(local, operators)
    applied = collect(again, targets, weight)
    return start, dual - applied
```

```python
import functools

import jax
import jax.numpy as jnp
from jax import lax
from jax.experimental import pallas as pl
from jax.experimental.pallas import tpu as pltpu
from jax.sharding import PartitionSpec as P

BLK = 128
LANES = 128
FLOWS = 4
AHEAD = 3
MESH = pl.DeviceIdType.MESH
VMEM_LIMIT = 62 * 1024 * 1024
F32 = jnp.float32
BF16 = jnp.bfloat16
I32 = jnp.int32


def flip(me, r, bits):
    out = me
    for b in range(bits):
        if (r >> b) & 1:
            out = out + (1 - 2 * (me // (1 << b) % 2)) * (1 << b)
    return out


def plan(bits, flows):
    rest = list(range(1, bits))
    return [[0] + (rest if f % 2 == 0 else rest[::-1]) for f in range(flows)]


def step_of(r, order):
    for t, b in enumerate(order):
        if (r >> b) & 1:
            return t
    return len(order)


def slot_table(n, order):
    table, done = {}, 0
    for t, b in enumerate(order):
        done |= 1 << b
        for r in range(n):
            if r & done == 0:
                table[(t, r)] = len(table)
    return table


def remote(src, dst, send_sem, recv_sem, peer):
    return pltpu.make_async_remote_copy(
        src_ref=src,
        dst_ref=dst,
        send_sem=send_sem,
        recv_sem=recv_sem,
        device_id={"sub": peer},
        device_id_type=MESH,
    )


class ReduceScatter:
    def __init__(self, n, bits, me, local, stage, recv, send_sem, recv_sem):
        self.n, self.bits, self.me, self.local = n, bits, me, local
        self.stage, self.recv = stage, recv
        self.send_sem, self.recv_sem = send_sem, recv_sem
        self.orders = plan(bits, FLOWS)
        self.tables = [slot_table(n, order) for order in self.orders]
        self.met = [False] * FLOWS

    def sem_of(self, f, slot):
        return self.recv_sem.at[f, max(0, slot - self.n // 2 + 1)]

    def wait(self, f, r, t):
        slot = self.tables[f][(t, r)]
        where = self.recv.at[f, slot]
        if t == 0:
            if self.met[f]:
                return
            self.met[f] = True
            where = self.recv.at[f, pl.ds(0, self.n // 2)]
        peer = flip(self.me, 1 << self.orders[f][t], self.bits)
        remote(where, where, self.send_sem, self.sem_of(f, slot), peer).wait_recv()

    def total(self, f, r, steps):
        part = self.local(f, flip(self.me, r, self.bits))
        for t in range(steps):
            self.wait(f, r, t)
            part = part + self.recv[f, self.tables[f][(t, r)]].astype(F32)
        return part

    def step(self, t, lands=None):
        group = []
        for f in range(FLOWS):
            for r in range(self.n):
                if step_of(r, self.orders[f]) == t:
                    land = r ^ (1 << self.orders[f][t])
                    when = step_of(land, self.orders[f])
                    if lands is None or when in lands:
                        group.append((f if t == 0 else 0, when, f, r, land))
        for _, _, f, r, land in sorted(group):
            self.stage[f, r - 1] = self.total(f, r, t).astype(BF16)
            slot = self.tables[f][(t, land)]
            peer = flip(self.me, 1 << self.orders[f][t], self.bits)
            remote(
                self.stage.at[f, r - 1],
                self.recv.at[f, slot],
                self.send_sem,
                self.sem_of(f, slot),
                peer,
            ).start()

    def finish(self, f):
        return self.total(f, 0, self.bits)

    def drain(self):
        peer = flip(self.me, 1, self.bits)
        remote(self.stage, self.recv, self.send_sem, self.recv_sem.at[0, 0], peer).wait_send()


class SumToAll:
    def __init__(self, n, bits, me, part, got, every, sems):
        self.n, self.bits, self.me = n, bits, me
        self.part, self.got, self.every, self.sems = part, got, every, sems
        self.groups, self.wide = part.shape[0], part.shape[2]
        self.rows = n // self.groups
        self.tall = part.shape[1] // self.rows

    def piece(self, ref, p):
        start = pl.multiple_of(p % self.rows * self.tall, self.tall)
        return ref.at[p // self.rows, pl.ds(start, self.tall)]

    def whole(self, way):
        where = self.got.at[pl.ds(1, self.n - 1)]
        peer = flip(self.me, 1, self.bits)
        return remote(where, where, self.sems.at[2 * way], self.sems.at[2 * way + 1], peer)

    def spread(self, acc):
        for c in range(self.groups):
            self.part[c] = acc[:, c * self.wide : (c + 1) * self.wide].astype(BF16)
        for r in range(1, self.n):
            peer = flip(self.me, r, self.bits)
            src, dst = self.piece(self.part, peer), self.got.at[r]
            remote(src, dst, self.sems.at[0], self.sems.at[1], peer).start()

    def gather(self):
        mine = self.piece(self.part, self.me)[...].astype(F32)
        self.whole(0).wait_recv()
        for r in range(1, self.n):
            mine = mine + self.got[r].astype(F32)
        where = self.piece(self.every, self.me)
        where[...] = mine.astype(BF16)
        for r in range(1, self.n):
            peer = flip(self.me, r, self.bits)
            remote(where, where, self.sems.at[2], self.sems.at[3], peer).start()

    def arrive(self):
        self.whole(1).wait_recv()

    def drain(self):
        self.whole(0).wait_send()
        self.whole(1).wait_send()


class AllGather:
    def __init__(self, n, bits, me, own_blocks, store, send_sem, recv_sem):
        self.n, self.bits, self.me = n, bits, me
        self.own_blocks, self.per = own_blocks, own_blocks // FLOWS
        self.store, self.send_sem, self.recv_sem = store, send_sem, recv_sem
        self.orders = [order[::-1] for order in plan(bits, FLOWS)]
        self.known = [[0] for _ in range(FLOWS)]

    def copy_of(self, f, r, land, b):
        base = flip(self.me, r, self.bits) * self.own_blocks + f * self.per
        where = self.store.at[pl.ds(base, self.per)]
        sem = self.recv_sem.at[0, 0] if land % 2 else self.recv_sem.at[f, land // 2]
        return remote(where, where, self.send_sem, sem, flip(self.me, 1 << b, self.bits))

    def send(self, f, r, u):
        for b in self.orders[f][u:]:
            self.copy_of(f, r, r ^ (1 << b), b).start()

    def begin(self, f):
        self.send(f, 0, 0)

    def step(self, u):
        for f in range(FLOWS):
            last = 1 << self.orders[f][u - 1]
            fresh = [r ^ last for r in self.known[f]]
            for r in fresh:
                self.copy_of(f, r, r, 1).wait_recv()
                self.send(f, r, u)
            self.known[f] = self.known[f] + fresh

    def whole(self, count):
        where = self.store.at[pl.ds(0, count * self.own_blocks)]
        peer = flip(self.me, 1, self.bits)
        return remote(where, where, self.send_sem, self.recv_sem.at[0, 0], peer)

    def arrive(self):
        self.whole(self.n // 2).wait_recv()

    def drain(self):
        self.whole(self.n - 1).wait_send()


def find_links(owner, block, own_blocks, index, duals):
    nblocks = owner.shape[1]
    target = owner[...] * own_blocks + block[...]
    rows = lax.broadcasted_iota(I32, (nblocks, nblocks), 0)
    cols = lax.broadcasted_iota(I32, (nblocks, nblocks), 1)
    wide = jnp.broadcast_to(target, (nblocks, nblocks))
    down = jnp.max(jnp.where(rows == cols, wide, -1), axis=1, keepdims=True)
    before = jnp.where((down == wide) & (rows < cols), rows, -1)
    before = jnp.max(before, axis=0, keepdims=True)
    names = lax.broadcasted_iota(I32, (nblocks, duals), 1)
    places = lax.broadcasted_iota(I32, (nblocks, duals), 0)
    last = jnp.max(jnp.where(down == names, places, -1), axis=0, keepdims=True)
    index[0:1, 0:nblocks] = target
    index[1:2, 0:nblocks] = jnp.where(before < 0, nblocks, before)
    index[2:3, 0:duals] = jnp.where(last < 0, nblocks, last)


def kernel(
    n,
    owner_ref,
    block_ref,
    scale,
    loads_hbm,
    operators_hbm,
    basis_hbm,
    coarse_hbm,
    start_hbm,
    resid_hbm,
    loads,
    operators,
    basis,
    coarse,
    runs,
    index,
    table,
    stage,
    recv,
    cacc,
    cpart,
    cgot,
    call,
    start_v,
    dual,
    in_sem,
    op_sem,
    load_sem,
    out_sem,
    send_sem,
    recv_sem,
    sum_sem,
    gsend_sem,
    grecv_sem,
    *gat,
):
    bits = n.bit_length() - 1
    me = lax.axis_index("sub")
    subs, columns, rows_in = loads.shape
    per_sub = rows_in // BLK
    nblocks = subs * per_sub
    chunks, (duals, high, _) = len(gat), gat[0].shape
    own_blocks = duals // n
    per = own_blocks // FLOWS
    flows = range(FLOWS)
    target = lambda i: table[0, i]
    before = lambda i: table[1, i]
    last = lambda i: table[2, i]

    barrier = pltpu.get_barrier_semaphore()
    for r in range(1, n):
        pl.semaphore_signal(
            barrier, inc=1, device_id={"sub": flip(me, r, bits)}, device_id_type=MESH
        )
    basis_copy = pltpu.make_async_copy(basis_hbm, basis, in_sem.at[0])
    coarse_copy = pltpu.make_async_copy(coarse_hbm, coarse, in_sem.at[1])
    table_copy = pltpu.make_async_copy(index, table, in_sem.at[2])

    def load_copy(s):
        return pltpu.make_async_copy(loads_hbm.at[s], loads.at[s], load_sem.at[s])

    def op_copy(s):
        return pltpu.make_async_copy(operators_hbm.at[s], operators.at[s], op_sem.at[s])

    ahead = min(AHEAD, subs)
    for s in range(ahead):
        load_copy(s).start()
        op_copy(s).start()
    find_links(owner_ref, block_ref, own_blocks, index, duals)
    table_copy.start()
    runs[nblocks] = jnp.zeros((columns, BLK), F32)
    weight = 1.0 / (1.0 + scale[...].astype(F32))
    table_copy.wait()

    def add_runs(s, span, prod):
        for j in range(per_sub):
            row = s * per_sub + j
            term = prod[:, j * BLK : (j + 1) * BLK].astype(BF16).astype(F32)
            runs[row, span] = term + runs[before(row), span]

    def first(s, carry):
        load_copy(s).wait()
        op_copy(s).wait()

        @pl.when(s + ahead < subs)
        def _():
            load_copy(s + ahead).start()
            op_copy(s + ahead).start()

        @pl.when(s + ahead == subs)
        def _():
            basis_copy.start()
            coarse_copy.start()

        add_runs(s, slice(None), jnp.dot(loads[s], operators[s], preferred_element_type=F32))
        return carry

    lax.fori_loop(0, subs, first, 0)
    pl.semaphore_wait(barrier, n - 1)

    spans = [slice(h * high, (h + 1) * high) for h in range(chunks)]

    def scatter_of(h):
        def local(f, owner):
            base = owner * own_blocks + f * per
            return jnp.stack([runs[last(base + i), spans[h]] for i in range(per)])

        return ReduceScatter(
            n, bits, me, local, stage.at[h], recv.at[h], send_sem.at[h], recv_sem.at[h]
        )

    one = [scatter_of(h) for h in range(chunks)]
    two = [scatter_of(h) for h in range(chunks)]
    sums = [
        SumToAll(
            n, bits, me, cpart.at[h], cgot.at[h], call.at[h], sum_sem.at[h]
        )
        for h in range(chunks)
    ]
    gathers = [
        AllGather(n, bits, me, own_blocks, gat[h], gsend_sem.at[h], grecv_sem.at[h])
        for h in range(chunks)
    ]

    def project(h):
        for f in flows:
            span = slice(f * per * BLK, (f + 1) * per * BLK)
            part = one[h].finish(f)
            pieces = []
            for i in range(per):
                blk = f * per + i
                pieces.append(part[i] * weight[blk : blk + 1, :])
            wide = jnp.concatenate(pieces, axis=1)
            dual[spans[h], span] = wide
            coeff = jnp.dot(wide.astype(BF16), basis[span], preferred_element_type=F32)
            if f == 0:
                cacc[h] = coeff
            else:
                cacc[h] += coeff
        sums[h].spread(cacc.at[h])

    def out_copy(h, which):
        src, dst = ((start_v, start_hbm), (dual, resid_hbm))[which]
        return pltpu.make_async_copy(src.at[spans[h]], dst.at[spans[h]], out_sem.at[h, which])

    def solve(h):
        sums[h].arrive()
        groups, width = call.shape[1], call.shape[3]
        solved = jnp.dot(call[h, 0], coarse[0:width], preferred_element_type=F32)
        for c in range(1, groups):
            solved = solved + jnp.dot(
                call[h, c], coarse[c * width : (c + 1) * width], preferred_element_type=F32
            )
        return solved.astype(BF16)

    def rise(h, solved, part_of):
        for f in part_of:
            span = slice(f * per * BLK, (f + 1) * per * BLK)
            part = lax.dot_general(
                solved, basis[span], (((1,), (1,)), ((), ())), preferred_element_type=F32
            )
            start_v[spans[h], span] = part
            for i in range(per):
                where = me * own_blocks + f * per + i
                gat[h][where] = part[:, i * BLK : (i + 1) * BLK].astype(BF16)
            gathers[h].begin(f)
            if f == FLOWS - 1:
                out_copy(h, 0).start()

    def apply(h, lo, hi):
        def second(s, carry):
            picked = [gat[h][target(s * per_sub + j)] for j in range(per_sub)]
            held = jnp.concatenate(picked, axis=1)
            prod = jnp.dot(held, operators[s], preferred_element_type=F32)
            add_runs(s, spans[h], prod)
            return carry

        lax.fori_loop(lo, hi, second, 0)

    def conclude(h):
        for f in flows:
            part = two[h].finish(f)
            for i in range(per):
                blk = f * per + i
                span = slice(blk * BLK, (blk + 1) * BLK)
                dual[spans[h], span] = (
                    dual[spans[h], span] - part[i] * weight[blk : blk + 1, :]
                )
        out_copy(h, 1).start()

    every = range(chunks)
    half = FLOWS // 2
    cut = [subs // 4, 3 * subs // 8, 7 * subs // 8]
    late, early = (bits,), tuple(range(bits))

    def wrap_up(h):
        one[h].drain()
        sums[h].drain()

    for h in every:
        one[h].step(0)
    basis_copy.wait()
    coarse_copy.wait()
    if chunks == 1:
        for t in range(1, bits):
            one[0].step(t)
        project(0)
        sums[0].gather()
        rise(0, solve(0), flows)
        for u in range(1, bits):
            gathers[0].step(u)
        gathers[0].arrive()
        wrap_up(0)
        apply(0, 0, subs)
        for t in range(bits):
            two[0].step(t)
        conclude(0)
    else:
        one[0].step(1)
        one[1].step(1, early)
        for t in range(2, bits):
            one[0].step(t)
        one[1].step(1, late)
        for t in range(2, bits):
            one[1].step(t)
        project(0)
        project(1)
        sums[0].gather()
        sums[1].gather()
        x0 = solve(0)
        rise(0, x0, flows)
        x1 = solve(1)
        rise(1, x1, flows[:half])
        gathers[0].step(1)
        rise(1, x1, flows[half:])
        for u in range(2, bits):
            gathers[0].step(u)
        wrap_up(0)
        gathers[1].step(1)
        gathers[0].arrive()
        apply(0, 0, cut[0])
        for u in range(2, bits):
            gathers[1].step(u)
        apply(0, cut[0], subs)
        two[0].step(0)
        wrap_up(1)
        gathers[1].arrive()
        apply(1, 0, cut[1])
        two[0].step(1)
        apply(1, cut[1], cut[2])
        for t in range(2, bits):
            two[0].step(t)
        apply(1, cut[2], subs)
        two[1].step(0)
        two[1].step(1)
        conclude(0)
        for t in range(2, bits):
            two[1].step(t)
        conclude(1)

    for h in range(chunks):
        for which in range(2):
            out_copy(h, which).wait()
        gathers[h].drain()
        two[h].drain()


def hand_over(start_in, resid_in, start_out, resid_out):
    start_out[...] = start_in[...]
    resid_out[...] = resid_in[...]


def chunks_of(n, columns, dirs):
    half = columns // 2
    groups = n // min(n, max(1, half // 16))
    return 2 if half % 16 == 0 and dirs // groups >= LANES else 1


def per_device(n, loads, operators, owner, dual_block, scale_index, basis, coarse):
    subs, columns, rows_in = loads.shape
    local_rows = basis.shape[0]
    own_blocks = local_rows // BLK
    duals = n * own_blocks
    nblocks = owner.shape[0]
    scale = scale_index.reshape(own_blocks, BLK)
    per = own_blocks // FLOWS
    dirs = coarse.shape[0]
    chunks = chunks_of(n, columns, dirs)
    high = columns // chunks
    rows = min(n, high // 16)
    groups = n // rows
    entries = max(LANES, duals)
    vmem = pl.BlockSpec(memory_space=pltpu.VMEM)
    hbm = pl.BlockSpec(memory_space=pl.ANY)
    dma = pltpu.SemaphoreType.DMA
    out = jax.ShapeDtypeStruct((columns, local_rows), F32)
    blocks = pltpu.VMEM((chunks, FLOWS, n - 1, per, high, BLK), BF16)
    results = pl.pallas_call(
        functools.partial(kernel, n),
        out_shape=(out, out),
        in_specs=[vmem, vmem, vmem] + [hbm] * 4,
        out_specs=(hbm, hbm),
        scratch_shapes=[
            pltpu.VMEM(loads.shape, BF16),
            pltpu.VMEM(operators.shape, BF16),
            pltpu.VMEM(basis.shape, BF16),
            pltpu.VMEM(coarse.shape, BF16),
            pltpu.VMEM((nblocks + 1, columns, BLK), F32),
            pltpu.VMEM((8, entries), I32),
            pltpu.SMEM((8, entries), I32),
            blocks,
            blocks,
            pltpu.VMEM((chunks, high, dirs), F32),
            pltpu.VMEM((chunks, groups, high, dirs // groups), BF16),
            pltpu.VMEM((chunks, n, high // rows, dirs // groups), BF16),
            pltpu.VMEM((chunks, groups, high, dirs // groups), BF16),
            pltpu.VMEM((columns, local_rows), F32),
            pltpu.VMEM((columns, local_rows), F32),
            dma((3,)),
            dma((subs,)),
            dma((subs,)),
            dma((chunks, 2)),
            dma((chunks,)),
            dma((chunks, FLOWS, n // 2)),
            dma((chunks, 4)),
            dma((chunks,)),
            dma((chunks, FLOWS, n // 2)),
        ]
        + [pltpu.VMEM((duals, high, BLK), BF16)] * chunks,
        compiler_params=pltpu.CompilerParams(
            collective_id=0, has_side_effects=True, vmem_limit_bytes=VMEM_LIMIT
        ),
        name="feti",
    )(
        owner.reshape(1, nblocks),
        dual_block.reshape(1, nblocks),
        scale,
        loads,
        operators,
        basis,
        coarse,
    )
    tile = pl.BlockSpec((columns // 2, local_rows), lambda i: (i, 0))
    return pl.pallas_call(
        hand_over,
        out_shape=(out, out),
        grid=(2,),
        in_specs=[tile, tile],
        out_specs=(tile, tile),
        name="hand_over",
    )(*results)


def solution(mesh):
    return jax.shard_map(
        functools.partial(per_device, mesh.shape["sub"]),
        mesh=mesh,
        in_specs=(
            P("sub", "rep", None),
            P("sub", None, None),
            P("sub", None),
            P("sub"),
            P("sub"),
            P("sub", None),
            P(),
        ),
        out_specs=(P("rep", "sub"), P("rep", "sub")),
        check_vma=False,
    )
```

```python
import functools

import jax
import jax.numpy as jnp
from jax import lax
from jax.experimental import pallas as pl
from jax.experimental.pallas import tpu as pltpu
from jax.sharding import PartitionSpec as P

BLK = 128
LANES = 128
FLOWS = 4
BY_FLOW = (0,)
CUTS = (2, 5, 1, 6)
AHEAD = 3
MESH = pl.DeviceIdType.MESH
VMEM_LIMIT = 55 * 1000 * 1000
F32 = jnp.float32
BF16 = jnp.bfloat16
I32 = jnp.int32


def flip(me, r, bits):
    out = me
    for b in range(bits):
        if (r >> b) & 1:
            out = out + (1 - 2 * (me // (1 << b) % 2)) * (1 << b)
    return out


def plan(bits, flows):
    rest = list(range(1, bits))
    return [[0] + (rest if f % 2 == 0 else rest[::-1]) for f in range(flows)]


def step_of(r, order):
    for t, b in enumerate(order):
        if (r >> b) & 1:
            return t
    return len(order)


def slot_table(n, order):
    table, done = {}, 0
    for t, b in enumerate(order):
        done |= 1 << b
        for r in range(n):
            if r & done == 0:
                table[(t, r)] = len(table)
    return table


def remote(src, dst, send_sem, recv_sem, peer):
    return pltpu.make_async_remote_copy(
        src_ref=src,
        dst_ref=dst,
        send_sem=send_sem,
        recv_sem=recv_sem,
        device_id={"sub": peer},
        device_id_type=MESH,
    )


class ReduceScatter:
    def __init__(self, n, bits, me, local, stage, recv, send_sem, recv_sem):
        self.n, self.bits, self.me, self.local = n, bits, me, local
        self.stage, self.recv = stage, recv
        self.send_sem, self.recv_sem = send_sem, recv_sem
        self.orders = plan(bits, FLOWS)
        self.tables = [slot_table(n, order) for order in self.orders]
        self.met = [False] * FLOWS

    def sem_of(self, f, slot):
        return self.recv_sem.at[f, max(0, slot - self.n // 2 + 1)]

    def wait(self, f, r, t):
        slot = self.tables[f][(t, r)]
        where = self.recv.at[f, slot]
        if t == 0:
            if self.met[f]:
                return
            self.met[f] = True
            where = self.recv.at[f, pl.ds(0, self.n // 2)]
        peer = flip(self.me, 1 << self.orders[f][t], self.bits)
        remote(where, where, self.send_sem, self.sem_of(f, slot), peer).wait_recv()

    def total(self, f, r, steps):
        part = self.local(f, flip(self.me, r, self.bits))
        for t in range(steps):
            self.wait(f, r, t)
            part = part + self.recv[f, self.tables[f][(t, r)]].astype(F32)
        return part

    def step(self, t, flows=range(FLOWS)):
        group = []
        for f in flows:
            for r in range(self.n):
                if step_of(r, self.orders[f]) == t:
                    land = r ^ (1 << self.orders[f][t])
                    when = step_of(land, self.orders[f])
                    group.append((f if t in BY_FLOW else 0, when, f, r, land))
        for _, _, f, r, land in sorted(group):
            self.stage[f, r - 1] = self.total(f, r, t).astype(BF16)
            slot = self.tables[f][(t, land)]
            peer = flip(self.me, 1 << self.orders[f][t], self.bits)
            remote(
                self.stage.at[f, r - 1],
                self.recv.at[f, slot],
                self.send_sem,
                self.sem_of(f, slot),
                peer,
            ).start()

    def finish(self, f):
        return self.total(f, 0, self.bits)

    def drain(self):
        peer = flip(self.me, 1, self.bits)
        remote(self.stage, self.recv, self.send_sem, self.recv_sem.at[0, 0], peer).wait_send()


class SumToAll:
    def __init__(self, n, bits, me, part, got, every, sems):
        self.n, self.bits, self.me = n, bits, me
        self.part, self.got, self.every, self.sems = part, got, every, sems
        self.groups, self.wide = part.shape[0], part.shape[2]
        self.rows = n // self.groups
        self.tall = part.shape[1] // self.rows

    def piece(self, ref, p):
        start = pl.multiple_of(p % self.rows * self.tall, self.tall)
        return ref.at[p // self.rows, pl.ds(start, self.tall)]

    def whole(self, way):
        where = self.got.at[pl.ds(1, self.n - 1)]
        peer = flip(self.me, 1, self.bits)
        return remote(where, where, self.sems.at[2 * way], self.sems.at[2 * way + 1], peer)

    def spread(self, acc):
        for c in range(self.groups):
            self.part[c] = acc[:, c * self.wide : (c + 1) * self.wide].astype(BF16)
        for r in range(1, self.n):
            peer = flip(self.me, r, self.bits)
            src, dst = self.piece(self.part, peer), self.got.at[r]
            remote(src, dst, self.sems.at[0], self.sems.at[1], peer).start()

    def gather(self):
        mine = self.piece(self.part, self.me)[...].astype(F32)
        self.whole(0).wait_recv()
        for r in range(1, self.n):
            mine = mine + self.got[r].astype(F32)
        where = self.piece(self.every, self.me)
        where[...] = mine.astype(BF16)
        for r in range(1, self.n):
            peer = flip(self.me, r, self.bits)
            remote(where, where, self.sems.at[2], self.sems.at[3], peer).start()

    def arrive(self):
        self.whole(1).wait_recv()

    def drain(self):
        self.whole(0).wait_send()
        self.whole(1).wait_send()


class AllGather:
    def __init__(self, n, bits, me, own_blocks, store, send_sem, recv_sem):
        self.n, self.bits, self.me = n, bits, me
        self.own_blocks, self.per = own_blocks, own_blocks // FLOWS
        self.store, self.send_sem, self.recv_sem = store, send_sem, recv_sem
        self.orders = [order[::-1] for order in plan(bits, FLOWS)]
        self.known = [[0] for _ in range(FLOWS)]

    def copy_of(self, f, r, land, b):
        base = flip(self.me, r, self.bits) * self.own_blocks + f * self.per
        where = self.store.at[pl.ds(base, self.per)]
        sem = self.recv_sem.at[0, 0] if land % 2 else self.recv_sem.at[f, land // 2]
        return remote(where, where, self.send_sem, sem, flip(self.me, 1 << b, self.bits))

    def send(self, f, r, u):
        for b in self.orders[f][u:]:
            self.copy_of(f, r, r ^ (1 << b), b).start()

    def begin(self, f):
        self.send(f, 0, 0)

    def step(self, u, flows=range(FLOWS)):
        for f in flows:
            last = 1 << self.orders[f][u - 1]
            fresh = [r ^ last for r in self.known[f]]
            for r in fresh:
                self.copy_of(f, r, r, 1).wait_recv()
                self.send(f, r, u)
            self.known[f] = self.known[f] + fresh

    def whole(self, count):
        where = self.store.at[pl.ds(0, count * self.own_blocks)]
        peer = flip(self.me, 1, self.bits)
        return remote(where, where, self.send_sem, self.recv_sem.at[0, 0], peer)

    def arrive(self):
        self.whole(self.n // 2).wait_recv()

    def drain(self):
        self.whole(self.n - 1).wait_send()


def find_links(target, index, duals):
    nblocks = target.shape[1]
    rows = lax.broadcasted_iota(I32, (nblocks, nblocks), 0)
    cols = lax.broadcasted_iota(I32, (nblocks, nblocks), 1)
    wide = jnp.broadcast_to(target, (nblocks, nblocks))
    down = jnp.max(jnp.where(rows == cols, wide, -1), axis=1, keepdims=True)
    before = jnp.where((down == wide) & (rows < cols), rows, -1)
    before = jnp.max(before, axis=0, keepdims=True)
    names = lax.broadcasted_iota(I32, (nblocks, duals), 1)
    places = lax.broadcasted_iota(I32, (nblocks, duals), 0)
    last = jnp.max(jnp.where(down == names, places, -1), axis=0, keepdims=True)
    index[0:1, 0:nblocks] = target
    index[1:2, 0:nblocks] = jnp.where(before < 0, nblocks, before)
    index[2:3, 0:duals] = jnp.where(last < 0, nblocks, last)


def kernel(
    n,
    meta,
    loads_hbm,
    operators_hbm,
    basis_hbm,
    coarse_hbm,
    start_hbm,
    resid_hbm,
    loads,
    operators,
    basis,
    coarse,
    runs,
    index,
    table,
    stage,
    recv,
    cacc,
    cpart,
    cgot,
    call,
    start_v,
    dual,
    in_sem,
    op_sem,
    load_sem,
    out_sem,
    send_sem,
    recv_sem,
    sum_sem,
    gsend_sem,
    grecv_sem,
    *gat,
):
    bits = n.bit_length() - 1
    me = lax.axis_index("sub")
    subs, columns, rows_in = loads.shape
    per_sub = rows_in // BLK
    nblocks = subs * per_sub
    chunks, (duals, high, _) = len(gat), gat[0].shape
    own_blocks = duals // n
    per = own_blocks // FLOWS
    flows = range(FLOWS)

    def target_of(i):
        return table[0, i]

    def before(i):
        return table[1, i]

    def last(i):
        return table[2, i]


    barrier = pltpu.get_barrier_semaphore()
    for r in range(1, n):
        pl.semaphore_signal(
            barrier, inc=1, device_id={"sub": flip(me, r, bits)}, device_id_type=MESH
        )
    basis_copy = pltpu.make_async_copy(basis_hbm, basis, in_sem.at[0])
    coarse_copy = pltpu.make_async_copy(coarse_hbm, coarse, in_sem.at[1])
    table_copy = pltpu.make_async_copy(index, table, in_sem.at[2])

    def load_copy(s):
        return pltpu.make_async_copy(loads_hbm.at[s], loads.at[s], load_sem.at[s])

    def op_copy(s):
        return pltpu.make_async_copy(operators_hbm.at[s], operators.at[s], op_sem.at[s])

    ahead = min(AHEAD, subs)
    for s in range(ahead):
        load_copy(s).start()
        op_copy(s).start()
    head = meta.shape[0] - own_blocks
    names = jnp.concatenate([meta[i : i + 1] for i in range(head)], axis=1)
    target = names[:, :nblocks] * own_blocks + names[:, nblocks : 2 * nblocks]
    find_links(target, index, duals)
    table_copy.start()
    runs[nblocks] = jnp.zeros((columns, BLK), F32)
    weight = 1.0 / (1.0 + meta[head:].astype(F32))
    table_copy.wait()

    def add_runs(s, span, prod):
        for j in range(per_sub):
            row = s * per_sub + j
            term = prod[:, j * BLK : (j + 1) * BLK].astype(BF16).astype(F32)
            runs[row, span] = term + runs[before(row), span]

    def first(s, carry):
        load_copy(s).wait()
        op_copy(s).wait()

        @pl.when(s + ahead < subs)
        def _():
            load_copy(s + ahead).start()
            op_copy(s + ahead).start()

        @pl.when(s + ahead == subs)
        def _():
            basis_copy.start()
            coarse_copy.start()

        add_runs(s, slice(None), jnp.dot(loads[s], operators[s], preferred_element_type=F32))
        return carry

    lax.fori_loop(0, subs, first, 0)
    pl.semaphore_wait(barrier, n - 1)

    spans = [slice(h * high, (h + 1) * high) for h in range(chunks)]

    def scatter_of(h):
        def local(f, owner):
            base = owner * own_blocks + f * per
            return jnp.stack([runs[last(base + i), spans[h]] for i in range(per)])

        return ReduceScatter(
            n, bits, me, local, stage.at[h], recv.at[h], send_sem.at[h], recv_sem.at[h]
        )

    one = [scatter_of(h) for h in range(chunks)]
    two = [scatter_of(h) for h in range(chunks)]
    sums = [
        SumToAll(
            n, bits, me, cpart.at[h], cgot.at[h], call.at[h], sum_sem.at[h]
        )
        for h in range(chunks)
    ]
    gathers = [
        AllGather(n, bits, me, own_blocks, gat[h], gsend_sem.at[h], grecv_sem.at[h])
        for h in range(chunks)
    ]

    def project(h):
        if h == 0:
            basis_copy.wait()
        for f in flows:
            span = slice(f * per * BLK, (f + 1) * per * BLK)
            part = one[h].finish(f)
            pieces = []
            for i in range(per):
                blk = f * per + i
                pieces.append(part[i] * weight[blk : blk + 1, :])
            wide = jnp.concatenate(pieces, axis=1)
            dual[spans[h], span] = wide
            coeff = jnp.dot(wide.astype(BF16), basis[span], preferred_element_type=F32)
            if f == 0:
                cacc[h] = coeff
            else:
                cacc[h] += coeff
        sums[h].spread(cacc.at[h])

    def out_copy(h, which):
        src, dst = ((start_v, start_hbm), (dual, resid_hbm))[which]
        return pltpu.make_async_copy(src.at[spans[h]], dst.at[spans[h]], out_sem.at[h, which])

    def solve(h):
        if h == 0:
            coarse_copy.wait()
        sums[h].arrive()
        groups, width = call.shape[1], call.shape[3]
        solved = jnp.dot(call[h, 0], coarse[0:width], preferred_element_type=F32)
        for c in range(1, groups):
            solved = solved + jnp.dot(
                call[h, c], coarse[c * width : (c + 1) * width], preferred_element_type=F32
            )
        return solved.astype(BF16)

    def rise(h, solved, part_of):
        for f in part_of:
            span = slice(f * per * BLK, (f + 1) * per * BLK)
            part = lax.dot_general(
                solved, basis[span], (((1,), (1,)), ((), ())), preferred_element_type=F32
            )
            start_v[spans[h], span] = part
            for i in range(per):
                where = me * own_blocks + f * per + i
                gat[h][where] = part[:, i * BLK : (i + 1) * BLK].astype(BF16)
            gathers[h].begin(f)
            if f == FLOWS - 1:
                out_copy(h, 0).start()

    def apply(h, lo, hi):
        def second(s, carry):
            picked = [gat[h][target_of(s * per_sub + j)] for j in range(per_sub)]
            held = jnp.concatenate(picked, axis=1)
            prod = jnp.dot(held, operators[s], preferred_element_type=F32)
            add_runs(s, spans[h], prod)
            return carry

        lax.fori_loop(lo, hi, second, 0)

    def conclude(h, some=range(FLOWS)):
        for f in some:
            part = two[h].finish(f)
            for i in range(per):
                blk = f * per + i
                span = slice(blk * BLK, (blk + 1) * BLK)
                dual[spans[h], span] = (
                    dual[spans[h], span] - part[i] * weight[blk : blk + 1, :]
                )
        if some[-1] == FLOWS - 1:
            out_copy(h, 1).start()

    every = range(chunks)
    half = FLOWS // 2
    cut = [subs * i // 8 for i in CUTS]

    def wrap_up(h):
        one[h].drain()
        sums[h].drain()

    for h in every:
        one[h].step(0)
    if chunks == 1:
        for t in range(1, bits):
            one[0].step(t)
        project(0)
        sums[0].gather()
        rise(0, solve(0), flows)
        for u in range(1, bits):
            gathers[0].step(u)
        gathers[0].arrive()
        wrap_up(0)
        apply(0, 0, subs)
        for t in range(bits):
            two[0].step(t)
        conclude(0)
    else:
        for t in range(1, bits):
            one[0].step(t)
        one[1].step(1)
        project(0)
        for t in range(2, bits):
            one[1].step(t)
        sums[0].gather()
        project(1)
        x0 = solve(0)
        rise(0, x0, flows[:half])
        sums[1].gather()
        rise(0, x0, flows[half:])
        gathers[0].step(1, flows[:-1])
        x1 = solve(1)
        gathers[0].step(1, flows[-1:])
        rise(1, x1, flows[:half])
        for f in flows[half:]:
            gathers[0].step(2, [f - half])
            rise(1, x1, [f])
        gathers[0].step(2, flows[half:])
        wrap_up(0)
        gathers[1].step(1, flows[:1])
        gathers[0].arrive()
        apply(0, 0, cut[0])
        gathers[1].step(1, flows[1:])
        apply(0, cut[0], cut[1])
        gathers[1].step(2, flows[:half])
        apply(0, cut[1], subs)
        gathers[1].step(2, flows[half:])
        two[0].step(0)
        wrap_up(1)
        gathers[1].arrive()
        apply(1, 0, cut[2])
        two[0].step(1)
        apply(1, cut[2], cut[3])
        two[0].step(2, flows[:half])
        apply(1, cut[3], subs)
        two[1].step(0)
        two[0].step(2, flows[half:])
        two[1].step(1)
        conclude(0)
        two[1].step(2)
        conclude(1)

    for h in range(chunks):
        for which in range(2):
            out_copy(h, which).wait()
        gathers[h].drain()
        two[h].drain()


def hand_over(start_in, resid_in, start_out, resid_out, sem):
    copies = [
        pltpu.make_async_copy(start_in, start_out, sem.at[0]),
        pltpu.make_async_copy(resid_in, resid_out, sem.at[1]),
    ]
    for copy in copies:
        copy.start()
    for copy in copies:
        copy.wait()


def chunks_of(n, columns, dirs):
    half = columns // 2
    groups = n // min(n, max(1, half // 16))
    return 2 if half % 16 == 0 and dirs // groups >= LANES else 1


def per_device(n, loads, operators, owner, dual_block, scale_index, basis, coarse):
    subs, columns, rows_in = loads.shape
    local_rows = basis.shape[0]
    own_blocks = local_rows // BLK
    duals = n * own_blocks
    nblocks = owner.shape[0]
    spare = jnp.zeros((-2 * nblocks % LANES,), I32)
    meta = jnp.concatenate([owner.reshape(-1), dual_block, spare, scale_index])
    meta = meta.reshape(-1, LANES)
    per = own_blocks // FLOWS
    dirs = coarse.shape[0]
    chunks = chunks_of(n, columns, dirs)
    high = columns // chunks
    rows = min(n, high // 16)
    groups = n // rows
    entries = max(LANES, duals)
    vmem = pl.BlockSpec(memory_space=pltpu.VMEM)
    hbm = pl.BlockSpec(memory_space=pl.ANY)
    dma = pltpu.SemaphoreType.DMA
    out = jax.ShapeDtypeStruct((columns, local_rows), F32)
    blocks = pltpu.VMEM((chunks, FLOWS, n - 1, per, high, BLK), BF16)
    results = pl.pallas_call(
        functools.partial(kernel, n),
        out_shape=(out, out),
        in_specs=[vmem] + [hbm] * 4,
        out_specs=(hbm, hbm),
        scratch_shapes=[
            pltpu.VMEM(loads.shape, BF16),
            pltpu.VMEM(operators.shape, BF16),
            pltpu.VMEM(basis.shape, BF16),
            pltpu.VMEM(coarse.shape, BF16),
            pltpu.VMEM((nblocks + 1, columns, BLK), F32),
            pltpu.VMEM((8, entries), I32),
            pltpu.SMEM((8, entries), I32),
            blocks,
            blocks,
            pltpu.VMEM((chunks, high, dirs), F32),
            pltpu.VMEM((chunks, groups, high, dirs // groups), BF16),
            pltpu.VMEM((chunks, n, high // rows, dirs // groups), BF16),
            pltpu.VMEM((chunks, groups, high, dirs // groups), BF16),
            pltpu.VMEM((columns, local_rows), F32),
            pltpu.VMEM((columns, local_rows), F32),
            dma((3,)),
            dma((subs,)),
            dma((subs,)),
            dma((chunks, 2)),
            dma((chunks,)),
            dma((chunks, FLOWS, n // 2)),
            dma((chunks, 4)),
            dma((chunks,)),
            dma((chunks, FLOWS, n // 2)),
        ]
        + [pltpu.VMEM((duals, high, BLK), BF16)] * chunks,
        compiler_params=pltpu.CompilerParams(
            collective_id=0, has_side_effects=True, vmem_limit_bytes=VMEM_LIMIT
        ),
        name="feti",
    )(
        meta,
        loads,
        operators,
        basis,
        coarse,
    )
    return pl.pallas_call(
        hand_over,
        out_shape=(out, out),
        in_specs=[vmem, vmem],
        out_specs=(hbm, hbm),
        scratch_shapes=[dma((2,))],
        compiler_params=pltpu.CompilerParams(vmem_limit_bytes=4 * out.size * 4),
        name="hand_over",
    )(*results)


def solution(mesh):
    return jax.shard_map(
        functools.partial(per_device, mesh.shape["sub"]),
        mesh=mesh,
        in_specs=(
            P("sub", "rep", None),
            P("sub", None, None),
            P("sub", None),
            P("sub"),
            P("sub"),
            P("sub", None),
            P(),
        ),
        out_specs=(P("rep", "sub"), P("rep", "sub")),
        check_vma=False,
    )
```

```python
import functools

import jax
import jax.numpy as jnp
from jax import lax
from jax.experimental import pallas as pl
from jax.experimental.pallas import tpu as pltpu
from jax.sharding import PartitionSpec as P

BLK = 128
LANES = 128
FLOWS = 4
BY_FLOW = (0,)
CUTS = (2, 5, 2, 8)
AHEAD = 3
MESH = pl.DeviceIdType.MESH
VMEM_LIMIT = 55 * 1000 * 1000
F32 = jnp.float32
BF16 = jnp.bfloat16
I32 = jnp.int32


def flip(me, r, bits):
    out = me
    for b in range(bits):
        if (r >> b) & 1:
            out = out + (1 - 2 * (me // (1 << b) % 2)) * (1 << b)
    return out


def plan(bits, flows):
    rest = list(range(1, bits))
    return [[0] + (rest if f % 2 == 0 else rest[::-1]) for f in range(flows)]


def step_of(r, order):
    for t, b in enumerate(order):
        if (r >> b) & 1:
            return t
    return len(order)


def slot_table(n, order):
    table, done = {}, 0
    for t, b in enumerate(order):
        done |= 1 << b
        for r in range(n):
            if r & done == 0:
                table[(t, r)] = len(table)
    return table


def remote(src, dst, send_sem, recv_sem, peer):
    return pltpu.make_async_remote_copy(
        src_ref=src,
        dst_ref=dst,
        send_sem=send_sem,
        recv_sem=recv_sem,
        device_id={"sub": peer},
        device_id_type=MESH,
    )


class ReduceScatter:
    def __init__(self, n, bits, me, local, stage, recv, send_sem, recv_sem):
        self.n, self.bits, self.me, self.local = n, bits, me, local
        self.stage, self.recv = stage, recv
        self.send_sem, self.recv_sem = send_sem, recv_sem
        self.orders = plan(bits, FLOWS)
        self.tables = [slot_table(n, order) for order in self.orders]
        self.met = [False] * FLOWS

    def sem_of(self, f, slot):
        return self.recv_sem.at[f, max(0, slot - self.n // 2 + 1)]

    def wait(self, f, r, t):
        slot = self.tables[f][(t, r)]
        where = self.recv.at[f, slot]
        if t == 0:
            if self.met[f]:
                return
            self.met[f] = True
            where = self.recv.at[f, pl.ds(0, self.n // 2)]
        peer = flip(self.me, 1 << self.orders[f][t], self.bits)
        remote(where, where, self.send_sem, self.sem_of(f, slot), peer).wait_recv()

    def total(self, f, r, steps):
        part = self.local(f, flip(self.me, r, self.bits))
        for t in range(steps):
            self.wait(f, r, t)
            part = part + self.recv[f, self.tables[f][(t, r)]].astype(F32)
        return part

    def step(self, t, flows=range(FLOWS)):
        group = []
        for f in flows:
            for r in range(self.n):
                if step_of(r, self.orders[f]) == t:
                    land = r ^ (1 << self.orders[f][t])
                    when = step_of(land, self.orders[f])
                    group.append((f if t in BY_FLOW else 0, when, f, r, land))
        for _, _, f, r, land in sorted(group):
            self.stage[f, r - 1] = self.total(f, r, t).astype(BF16)
            slot = self.tables[f][(t, land)]
            peer = flip(self.me, 1 << self.orders[f][t], self.bits)
            remote(
                self.stage.at[f, r - 1],
                self.recv.at[f, slot],
                self.send_sem,
                self.sem_of(f, slot),
                peer,
            ).start()

    def finish(self, f):
        return self.total(f, 0, self.bits)

    def drain(self):
        peer = flip(self.me, 1, self.bits)
        remote(self.stage, self.recv, self.send_sem, self.recv_sem.at[0, 0], peer).wait_send()


class SumToAll:
    def __init__(self, n, bits, me, part, got, every, sems):
        self.n, self.bits, self.me = n, bits, me
        self.part, self.got, self.every, self.sems = part, got, every, sems
        self.groups, self.wide = part.shape[0], part.shape[2]
        self.rows = n // self.groups
        self.tall = part.shape[1] // self.rows

    def piece(self, ref, p):
        start = pl.multiple_of(p % self.rows * self.tall, self.tall)
        return ref.at[p // self.rows, pl.ds(start, self.tall)]

    def whole(self, way):
        where = self.got.at[pl.ds(1, self.n - 1)]
        peer = flip(self.me, 1, self.bits)
        return remote(where, where, self.sems.at[2 * way], self.sems.at[2 * way + 1], peer)

    def spread(self, acc):
        for c in range(self.groups):
            self.part[c] = acc[:, c * self.wide : (c + 1) * self.wide].astype(BF16)
        for r in range(1, self.n):
            peer = flip(self.me, r, self.bits)
            src, dst = self.piece(self.part, peer), self.got.at[r]
            remote(src, dst, self.sems.at[0], self.sems.at[1], peer).start()

    def gather(self):
        mine = self.piece(self.part, self.me)[...].astype(F32)
        self.whole(0).wait_recv()
        for r in range(1, self.n):
            mine = mine + self.got[r].astype(F32)
        where = self.piece(self.every, self.me)
        where[...] = mine.astype(BF16)
        for r in range(1, self.n):
            peer = flip(self.me, r, self.bits)
            remote(where, where, self.sems.at[2], self.sems.at[3], peer).start()

    def arrive(self):
        self.whole(1).wait_recv()

    def drain(self):
        self.whole(0).wait_send()
        self.whole(1).wait_send()


class AllGather:
    def __init__(self, n, bits, me, own_blocks, store, send_sem, recv_sem):
        self.n, self.bits, self.me = n, bits, me
        self.own_blocks, self.per = own_blocks, own_blocks // FLOWS
        self.store, self.send_sem, self.recv_sem = store, send_sem, recv_sem
        self.orders = [order[::-1] for order in plan(bits, FLOWS)]
        self.known = [[0] for _ in range(FLOWS)]

    def copy_of(self, f, r, land, b):
        base = flip(self.me, r, self.bits) * self.own_blocks + f * self.per
        where = self.store.at[pl.ds(base, self.per)]
        sem = self.recv_sem.at[0, 0] if land % 2 else self.recv_sem.at[f, land // 2]
        return remote(where, where, self.send_sem, sem, flip(self.me, 1 << b, self.bits))

    def send(self, f, r, u):
        for b in self.orders[f][u:]:
            self.copy_of(f, r, r ^ (1 << b), b).start()

    def begin(self, f):
        self.send(f, 0, 0)

    def step(self, u, flows=range(FLOWS)):
        for f in flows:
            last = 1 << self.orders[f][u - 1]
            fresh = [r ^ last for r in self.known[f]]
            for r in fresh:
                self.copy_of(f, r, r, 1).wait_recv()
                self.send(f, r, u)
            self.known[f] = self.known[f] + fresh

    def whole(self, count):
        where = self.store.at[pl.ds(0, count * self.own_blocks)]
        peer = flip(self.me, 1, self.bits)
        return remote(where, where, self.send_sem, self.recv_sem.at[0, 0], peer)

    def arrive(self):
        self.whole(self.n // 2).wait_recv()

    def drain(self):
        self.whole(self.n - 1).wait_send()


def find_links(target, index, duals):
    nblocks = target.shape[1]
    rows = lax.broadcasted_iota(I32, (nblocks, nblocks), 0)
    cols = lax.broadcasted_iota(I32, (nblocks, nblocks), 1)
    wide = jnp.broadcast_to(target, (nblocks, nblocks))
    down = jnp.max(jnp.where(rows == cols, wide, -1), axis=1, keepdims=True)
    before = jnp.where((down == wide) & (rows < cols), rows, -1)
    before = jnp.max(before, axis=0, keepdims=True)
    names = lax.broadcasted_iota(I32, (nblocks, duals), 1)
    places = lax.broadcasted_iota(I32, (nblocks, duals), 0)
    last = jnp.max(jnp.where(down == names, places, -1), axis=0, keepdims=True)
    index[0:1, 0:nblocks] = target
    index[1:2, 0:nblocks] = jnp.where(before < 0, nblocks, before)
    index[2:3, 0:duals] = jnp.where(last < 0, nblocks, last)


def kernel(
    n,
    meta,
    loads_hbm,
    operators_hbm,
    basis_hbm,
    coarse_hbm,
    start_ref,
    resid_ref,
    loads,
    operators,
    basis,
    coarse,
    runs,
    index,
    table,
    stage,
    recv,
    cacc,
    cpart,
    cgot,
    call,
    dual,
    in_sem,
    op_sem,
    load_sem,
    send_sem,
    recv_sem,
    sum_sem,
    gsend_sem,
    grecv_sem,
    *gat,
):
    bits = n.bit_length() - 1
    me = lax.axis_index("sub")
    subs, columns, rows_in = loads.shape
    per_sub = rows_in // BLK
    nblocks = subs * per_sub
    chunks, (duals, high, _) = len(gat), gat[0].shape
    own_blocks = duals // n
    per = own_blocks // FLOWS
    flows = range(FLOWS)

    def target_of(i):
        return table[0, i]

    def before(i):
        return table[1, i]

    def last(i):
        return table[2, i]


    barrier = pltpu.get_barrier_semaphore()
    for r in range(1, n):
        pl.semaphore_signal(
            barrier, inc=1, device_id={"sub": flip(me, r, bits)}, device_id_type=MESH
        )
    basis_copy = pltpu.make_async_copy(basis_hbm, basis, in_sem.at[0])
    coarse_copy = pltpu.make_async_copy(coarse_hbm, coarse, in_sem.at[1])
    table_copy = pltpu.make_async_copy(index, table, in_sem.at[2])

    def load_copy(s):
        return pltpu.make_async_copy(loads_hbm.at[s], loads.at[s], load_sem.at[s])

    def op_copy(s):
        return pltpu.make_async_copy(operators_hbm.at[s], operators.at[s], op_sem.at[s])

    ahead = min(AHEAD, subs)
    for s in range(ahead):
        load_copy(s).start()
        op_copy(s).start()
    head = meta.shape[0] - own_blocks
    names = jnp.concatenate([meta[i : i + 1] for i in range(head)], axis=1)
    target = names[:, :nblocks] * own_blocks + names[:, nblocks : 2 * nblocks]
    find_links(target, index, duals)
    table_copy.start()
    runs[nblocks] = jnp.zeros((columns, BLK), F32)
    weight = 1.0 / (1.0 + meta[head:].astype(F32))
    table_copy.wait()

    def add_runs(s, span, prod):
        for j in range(per_sub):
            row = s * per_sub + j
            term = prod[:, j * BLK : (j + 1) * BLK].astype(BF16).astype(F32)
            runs[row, span] = term + runs[before(row), span]

    def first(s, carry):
        load_copy(s).wait()
        op_copy(s).wait()

        @pl.when(s + ahead < subs)
        def _():
            load_copy(s + ahead).start()
            op_copy(s + ahead).start()

        @pl.when(s + ahead == subs)
        def _():
            basis_copy.start()
            coarse_copy.start()

        add_runs(s, slice(None), jnp.dot(loads[s], operators[s], preferred_element_type=F32))
        return carry

    lax.fori_loop(0, subs, first, 0)
    pl.semaphore_wait(barrier, n - 1)

    spans = [slice(h * high, (h + 1) * high) for h in range(chunks)]

    def scatter_of(h):
        def local(f, owner):
            base = owner * own_blocks + f * per
            return jnp.stack([runs[last(base + i), spans[h]] for i in range(per)])

        return ReduceScatter(
            n, bits, me, local, stage.at[h], recv.at[h], send_sem.at[h], recv_sem.at[h]
        )

    one = [scatter_of(h) for h in range(chunks)]
    two = [scatter_of(h) for h in range(chunks)]
    sums = [
        SumToAll(
            n, bits, me, cpart.at[h], cgot.at[h], call.at[h], sum_sem.at[h]
        )
        for h in range(chunks)
    ]
    gathers = [
        AllGather(n, bits, me, own_blocks, gat[h], gsend_sem.at[h], grecv_sem.at[h])
        for h in range(chunks)
    ]

    def project(h):
        if h == 0:
            basis_copy.wait()
        for f in flows:
            span = slice(f * per * BLK, (f + 1) * per * BLK)
            part = one[h].finish(f)
            pieces = []
            for i in range(per):
                blk = f * per + i
                pieces.append(part[i] * weight[blk : blk + 1, :])
            wide = jnp.concatenate(pieces, axis=1)
            dual[spans[h], span] = wide
            coeff = jnp.dot(wide.astype(BF16), basis[span], preferred_element_type=F32)
            if f == 0:
                cacc[h] = coeff
            else:
                cacc[h] += coeff
        sums[h].spread(cacc.at[h])

    def solve(h):
        if h == 0:
            coarse_copy.wait()
        sums[h].arrive()
        groups, width = call.shape[1], call.shape[3]
        solved = jnp.dot(call[h, 0], coarse[0:width], preferred_element_type=F32)
        for c in range(1, groups):
            solved = solved + jnp.dot(
                call[h, c], coarse[c * width : (c + 1) * width], preferred_element_type=F32
            )
        return solved.astype(BF16)

    def rise(h, solved, part_of):
        for f in part_of:
            span = slice(f * per * BLK, (f + 1) * per * BLK)
            part = lax.dot_general(
                solved, basis[span], (((1,), (1,)), ((), ())), preferred_element_type=F32
            )
            start_ref[spans[h], span] = part
            for i in range(per):
                where = me * own_blocks + f * per + i
                gat[h][where] = part[:, i * BLK : (i + 1) * BLK].astype(BF16)
            gathers[h].begin(f)

    def apply(h, lo, hi):
        def second(s, carry):
            picked = [gat[h][target_of(s * per_sub + j)] for j in range(per_sub)]
            held = jnp.concatenate(picked, axis=1)
            prod = jnp.dot(held, operators[s], preferred_element_type=F32)
            add_runs(s, spans[h], prod)
            return carry

        lax.fori_loop(lo, hi, second, 0)

    def conclude(h):
        for f in flows:
            part = two[h].finish(f)
            for i in range(per):
                blk = f * per + i
                span = slice(blk * BLK, (blk + 1) * BLK)
                resid_ref[spans[h], span] = (
                    dual[spans[h], span] - part[i] * weight[blk : blk + 1, :]
                )

    every = range(chunks)
    half = FLOWS // 2
    cut = [subs * i // 8 for i in CUTS]

    def wrap_up(h):
        one[h].drain()
        sums[h].drain()

    for h in every:
        one[h].step(0)
    if chunks == 1:
        for t in range(1, bits):
            one[0].step(t)
        project(0)
        sums[0].gather()
        rise(0, solve(0), flows)
        for u in range(1, bits):
            gathers[0].step(u)
        gathers[0].arrive()
        wrap_up(0)
        apply(0, 0, subs)
        for t in range(bits):
            two[0].step(t)
        conclude(0)
    else:
        for t in range(1, bits):
            one[0].step(t)
        one[1].step(1)
        project(0)
        for t in range(2, bits):
            one[1].step(t)
        sums[0].gather()
        project(1)
        x0 = solve(0)
        rise(0, x0, flows[:half])
        sums[1].gather()
        rise(0, x0, flows[half:])
        gathers[0].step(1)
        x1 = solve(1)
        rise(1, x1, flows[:half])
        gathers[0].step(2, flows[:half])
        rise(1, x1, flows[half:])
        gathers[0].step(2, flows[half:])
        wrap_up(0)
        gathers[0].arrive()
        apply(0, 0, cut[0])
        gathers[1].step(1)
        apply(0, cut[0], cut[1])
        gathers[1].step(2, flows[:half])
        apply(0, cut[1], subs)
        gathers[1].step(2, flows[half:])
        two[0].step(0)
        wrap_up(1)
        gathers[1].arrive()
        apply(1, 0, cut[2])
        two[0].step(1)
        apply(1, cut[2], cut[3])
        two[0].step(2, flows[:half])
        apply(1, cut[3], subs)
        two[1].step(0)
        two[0].step(2, flows[half:])
        two[1].step(1)
        conclude(0)
        two[1].step(2)
        conclude(1)

    for h in range(chunks):
        gathers[h].drain()
        two[h].drain()


def hand_over(start_in, resid_in, start_out, resid_out, sem):
    copies = [
        pltpu.make_async_copy(start_in, start_out, sem.at[0]),
        pltpu.make_async_copy(resid_in, resid_out, sem.at[1]),
    ]
    for copy in copies:
        copy.start()
    for copy in copies:
        copy.wait()


def chunks_of(n, columns, dirs):
    half = columns // 2
    groups = n // min(n, max(1, half // 16))
    return 2 if half % 16 == 0 and dirs // groups >= LANES else 1


def per_device(n, loads, operators, owner, dual_block, scale_index, basis, coarse):
    subs, columns, rows_in = loads.shape
    local_rows = basis.shape[0]
    own_blocks = local_rows // BLK
    duals = n * own_blocks
    nblocks = owner.shape[0]
    spare = jnp.zeros((-2 * nblocks % LANES,), I32)
    meta = jnp.concatenate([owner.reshape(-1), dual_block, spare, scale_index])
    meta = meta.reshape(-1, LANES)
    per = own_blocks // FLOWS
    dirs = coarse.shape[0]
    chunks = chunks_of(n, columns, dirs)
    high = columns // chunks
    rows = min(n, high // 16)
    groups = n // rows
    entries = max(LANES, duals)
    vmem = pl.BlockSpec(memory_space=pltpu.VMEM)
    hbm = pl.BlockSpec(memory_space=pl.ANY)
    dma = pltpu.SemaphoreType.DMA
    out = jax.ShapeDtypeStruct((columns, local_rows), F32)
    blocks = pltpu.VMEM((chunks, FLOWS, n - 1, per, high, BLK), BF16)
    results = pl.pallas_call(
        functools.partial(kernel, n),
        out_shape=(out, out),
        in_specs=[vmem] + [hbm] * 4,
        out_specs=(vmem, vmem),
        scratch_shapes=[
            pltpu.VMEM(loads.shape, BF16),
            pltpu.VMEM(operators.shape, BF16),
            pltpu.VMEM(basis.shape, BF16),
            pltpu.VMEM(coarse.shape, BF16),
            pltpu.VMEM((nblocks + 1, columns, BLK), F32),
            pltpu.VMEM((8, entries), I32),
            pltpu.SMEM((8, entries), I32),
            blocks,
            blocks,
            pltpu.VMEM((chunks, high, dirs), F32),
            pltpu.VMEM((chunks, groups, high, dirs // groups), BF16),
            pltpu.VMEM((chunks, n, high // rows, dirs // groups), BF16),
            pltpu.VMEM((chunks, groups, high, dirs // groups), BF16),
            pltpu.VMEM((columns, local_rows), F32),
            dma((3,)),
            dma((subs,)),
            dma((subs,)),
            dma((chunks,)),
            dma((chunks, FLOWS, n // 2)),
            dma((chunks, 4)),
            dma((chunks,)),
            dma((chunks, FLOWS, n // 2)),
        ]
        + [pltpu.VMEM((duals, high, BLK), BF16)] * chunks,
        compiler_params=pltpu.CompilerParams(
            collective_id=0, has_side_effects=True, vmem_limit_bytes=VMEM_LIMIT
        ),
        name="feti",
    )(
        meta,
        loads,
        operators,
        basis,
        coarse,
    )
    return pl.pallas_call(
        hand_over,
        out_shape=(out, out),
        in_specs=[vmem, vmem],
        out_specs=(hbm, hbm),
        scratch_shapes=[dma((2,))],
        compiler_params=pltpu.CompilerParams(vmem_limit_bytes=4 * out.size * 4),
        name="hand_over",
    )(*results)


def solution(mesh):
    return jax.shard_map(
        functools.partial(per_device, mesh.shape["sub"]),
        mesh=mesh,
        in_specs=(
            P("sub", "rep", None),
            P("sub", None, None),
            P("sub", None),
            P("sub"),
            P("sub"),
            P("sub", None),
            P(),
        ),
        out_specs=(P("rep", "sub"), P("rep", "sub")),
        check_vma=False,
    )
```

```python
import functools

import jax
import jax.numpy as jnp
from jax import lax
from jax.experimental import pallas as pl
from jax.experimental.pallas import tpu as pltpu
from jax.sharding import PartitionSpec as P

BLK = 128
LANES = 128
FLOWS = 4
BY_FLOW = (0,)
CUTS = (2, 5, 2)
AHEAD = 3
MESH = pl.DeviceIdType.MESH
VMEM_LIMIT = 55 * 1000 * 1000
F32 = jnp.float32
BF16 = jnp.bfloat16
I32 = jnp.int32


def flip(me, r, bits):
    out = me
    for b in range(bits):
        if (r >> b) & 1:
            out = out + (1 - 2 * (me // (1 << b) % 2)) * (1 << b)
    return out


def plan(bits, flows):
    rest = list(range(1, bits))
    return [[0] + (rest if f % 2 == 0 else rest[::-1]) for f in range(flows)]


def step_of(r, order):
    for t, b in enumerate(order):
        if (r >> b) & 1:
            return t
    return len(order)


def slot_table(n, order):
    table, done = {}, 0
    for t, b in enumerate(order):
        done |= 1 << b
        for r in range(n):
            if r & done == 0:
                table[(t, r)] = len(table)
    return table


def remote(src, dst, send_sem, recv_sem, peer):
    return pltpu.make_async_remote_copy(
        src_ref=src,
        dst_ref=dst,
        send_sem=send_sem,
        recv_sem=recv_sem,
        device_id={"sub": peer},
        device_id_type=MESH,
    )


class ReduceScatter:
    def __init__(self, n, bits, me, local, stage, recv, send_sem, recv_sem):
        self.n, self.bits, self.me, self.local = n, bits, me, local
        self.stage, self.recv = stage, recv
        self.send_sem, self.recv_sem = send_sem, recv_sem
        self.orders = plan(bits, FLOWS)
        self.tables = [slot_table(n, order) for order in self.orders]
        self.met = [False] * FLOWS

    def sem_of(self, f, slot):
        return self.recv_sem.at[f, max(0, slot - self.n // 2 + 1)]

    def wait(self, f, r, t):
        slot = self.tables[f][(t, r)]
        where = self.recv.at[f, slot]
        if t == 0:
            if self.met[f]:
                return
            self.met[f] = True
            where = self.recv.at[f, pl.ds(0, self.n // 2)]
        peer = flip(self.me, 1 << self.orders[f][t], self.bits)
        remote(where, where, self.send_sem, self.sem_of(f, slot), peer).wait_recv()

    def total(self, f, r, steps):
        part = self.local(f, flip(self.me, r, self.bits))
        for t in range(steps):
            self.wait(f, r, t)
            part = part + self.recv[f, self.tables[f][(t, r)]].astype(F32)
        return part

    def step(self, t, flows=range(FLOWS)):
        group = []
        for f in flows:
            for r in range(self.n):
                if step_of(r, self.orders[f]) == t:
                    land = r ^ (1 << self.orders[f][t])
                    when = step_of(land, self.orders[f])
                    group.append((f if t in BY_FLOW else 0, when, f, r, land))
        for _, _, f, r, land in sorted(group):
            self.stage[f, r - 1] = self.total(f, r, t).astype(BF16)
            slot = self.tables[f][(t, land)]
            peer = flip(self.me, 1 << self.orders[f][t], self.bits)
            remote(
                self.stage.at[f, r - 1],
                self.recv.at[f, slot],
                self.send_sem,
                self.sem_of(f, slot),
                peer,
            ).start()

    def finish(self, f):
        return self.total(f, 0, self.bits)

    def drain(self):
        peer = flip(self.me, 1, self.bits)
        remote(self.stage, self.recv, self.send_sem, self.recv_sem.at[0, 0], peer).wait_send()


class SumToAll:
    def __init__(self, n, bits, me, part, got, every, sems):
        self.n, self.bits, self.me = n, bits, me
        self.part, self.got, self.every, self.sems = part, got, every, sems
        self.groups, self.wide = part.shape[0], part.shape[2]
        self.rows = n // self.groups
        self.tall = part.shape[1] // self.rows

    def piece(self, ref, p):
        start = pl.multiple_of(p % self.rows * self.tall, self.tall)
        return ref.at[p // self.rows, pl.ds(start, self.tall)]

    def whole(self, way):
        where = self.got.at[pl.ds(1, self.n - 1)]
        peer = flip(self.me, 1, self.bits)
        return remote(where, where, self.sems.at[2 * way], self.sems.at[2 * way + 1], peer)

    def spread(self, acc):
        for c in range(self.groups):
            self.part[c] = acc[:, c * self.wide : (c + 1) * self.wide].astype(BF16)
        for r in reversed(range(1, self.n)):
            peer = flip(self.me, r, self.bits)
            src, dst = self.piece(self.part, peer), self.got.at[r]
            remote(src, dst, self.sems.at[0], self.sems.at[1], peer).start()

    def gather(self):
        mine = self.piece(self.part, self.me)[...].astype(F32)
        self.whole(0).wait_recv()
        for r in range(1, self.n):
            mine = mine + self.got[r].astype(F32)
        where = self.piece(self.every, self.me)
        where[...] = mine.astype(BF16)
        for r in reversed(range(1, self.n)):
            peer = flip(self.me, r, self.bits)
            remote(where, where, self.sems.at[2], self.sems.at[3], peer).start()

    def arrive(self):
        self.whole(1).wait_recv()

    def drain(self):
        self.whole(0).wait_send()
        self.whole(1).wait_send()


class AllGather:
    def __init__(self, n, bits, me, own_blocks, store, send_sem, recv_sem):
        self.n, self.bits, self.me = n, bits, me
        self.own_blocks, self.per = own_blocks, own_blocks // FLOWS
        self.store, self.send_sem, self.recv_sem = store, send_sem, recv_sem
        self.orders = [order[::-1] for order in plan(bits, FLOWS)]
        self.known = [[0] for _ in range(FLOWS)]

    def copy_of(self, f, r, land, b):
        base = flip(self.me, r, self.bits) * self.own_blocks + f * self.per
        where = self.store.at[pl.ds(base, self.per)]
        sem = self.recv_sem.at[0, 0] if land % 2 else self.recv_sem.at[f, land // 2]
        return remote(where, where, self.send_sem, sem, flip(self.me, 1 << b, self.bits))

    def send(self, f, r, u):
        for b in self.orders[f][u:]:
            self.copy_of(f, r, r ^ (1 << b), b).start()

    def begin(self, f):
        self.send(f, 0, 0)

    def step(self, u, flows=range(FLOWS)):
        for f in flows:
            last = 1 << self.orders[f][u - 1]
            fresh = [r ^ last for r in self.known[f]]
            for r in fresh:
                self.copy_of(f, r, r, 1).wait_recv()
                self.send(f, r, u)
            self.known[f] = self.known[f] + fresh

    def whole(self, count):
        where = self.store.at[pl.ds(0, count * self.own_blocks)]
        peer = flip(self.me, 1, self.bits)
        return remote(where, where, self.send_sem, self.recv_sem.at[0, 0], peer)

    def arrive(self):
        self.whole(self.n // 2).wait_recv()

    def drain(self):
        self.whole(self.n - 1).wait_send()


def find_links(target, index, duals):
    nblocks = target.shape[1]
    rows = lax.broadcasted_iota(I32, (nblocks, nblocks), 0)
    cols = lax.broadcasted_iota(I32, (nblocks, nblocks), 1)
    wide = jnp.broadcast_to(target, (nblocks, nblocks))
    down = jnp.max(jnp.where(rows == cols, wide, -1), axis=1, keepdims=True)
    before = jnp.where((down == wide) & (rows < cols), rows, -1)
    before = jnp.max(before, axis=0, keepdims=True)
    names = lax.broadcasted_iota(I32, (nblocks, duals), 1)
    places = lax.broadcasted_iota(I32, (nblocks, duals), 0)
    last = jnp.max(jnp.where(down == names, places, -1), axis=0, keepdims=True)
    index[0:1, 0:nblocks] = target
    index[1:2, 0:nblocks] = jnp.where(before < 0, nblocks, before)
    index[2:3, 0:duals] = jnp.where(last < 0, nblocks, last)


def kernel(
    n,
    meta,
    loads_hbm,
    operators_hbm,
    basis_hbm,
    coarse_hbm,
    start_ref,
    resid_ref,
    loads,
    operators,
    basis,
    coarse,
    runs,
    index,
    table,
    stage,
    recv,
    cacc,
    cpart,
    cgot,
    call,
    dual,
    in_sem,
    op_sem,
    load_sem,
    send_sem,
    recv_sem,
    sum_sem,
    gsend_sem,
    grecv_sem,
    *gat,
):
    bits = n.bit_length() - 1
    me = lax.axis_index("sub")
    subs, columns, rows_in = loads.shape
    per_sub = rows_in // BLK
    nblocks = subs * per_sub
    chunks, (duals, high, _) = len(gat), gat[0].shape
    own_blocks = duals // n
    per = own_blocks // FLOWS
    flows = range(FLOWS)

    def target_of(i):
        return table[0, i]

    def before(i):
        return table[1, i]

    def last(i):
        return table[2, i]


    barrier = pltpu.get_barrier_semaphore()
    for r in range(1, n):
        pl.semaphore_signal(
            barrier, inc=1, device_id={"sub": flip(me, r, bits)}, device_id_type=MESH
        )
    basis_copy = pltpu.make_async_copy(basis_hbm, basis, in_sem.at[0])
    coarse_copy = pltpu.make_async_copy(coarse_hbm, coarse, in_sem.at[1])
    table_copy = pltpu.make_async_copy(index, table, in_sem.at[2])

    def load_copy(s):
        return pltpu.make_async_copy(loads_hbm.at[s], loads.at[s], load_sem.at[s])

    def op_copy(s):
        return pltpu.make_async_copy(operators_hbm.at[s], operators.at[s], op_sem.at[s])

    ahead = min(AHEAD, subs)
    for s in range(ahead):
        load_copy(s).start()
        op_copy(s).start()
    head = meta.shape[0] - own_blocks
    names = jnp.concatenate([meta[i : i + 1] for i in range(head)], axis=1)
    target = names[:, :nblocks] * own_blocks + names[:, nblocks : 2 * nblocks]
    find_links(target, index, duals)
    table_copy.start()
    runs[nblocks] = jnp.zeros((columns, BLK), F32)
    weight = 1.0 / (1.0 + meta[head:].astype(F32))
    table_copy.wait()

    def add_runs(s, span, prod):
        for j in range(per_sub):
            row = s * per_sub + j
            term = prod[:, j * BLK : (j + 1) * BLK].astype(BF16).astype(F32)
            runs[row, span] = term + runs[before(row), span]

    def first(s, carry):
        load_copy(s).wait()
        op_copy(s).wait()

        @pl.when(s + ahead < subs)
        def _():
            load_copy(s + ahead).start()
            op_copy(s + ahead).start()

        @pl.when(s + ahead == subs)
        def _():
            basis_copy.start()
            coarse_copy.start()

        add_runs(s, slice(None), jnp.dot(loads[s], operators[s], preferred_element_type=F32))
        return carry

    lax.fori_loop(0, subs, first, 0)
    pl.semaphore_wait(barrier, n - 1)

    spans = [slice(h * high, (h + 1) * high) for h in range(chunks)]

    def scatter_of(h):
        def local(f, owner):
            base = owner * own_blocks + f * per
            return jnp.stack([runs[last(base + i), spans[h]] for i in range(per)])

        return ReduceScatter(
            n, bits, me, local, stage.at[h], recv.at[h], send_sem.at[h], recv_sem.at[h]
        )

    one = [scatter_of(h) for h in range(chunks)]
    two = [scatter_of(h) for h in range(chunks)]
    sums = [
        SumToAll(
            n, bits, me, cpart.at[h], cgot.at[h], call.at[h], sum_sem.at[h]
        )
        for h in range(chunks)
    ]
    gathers = [
        AllGather(n, bits, me, own_blocks, gat[h], gsend_sem.at[h], grecv_sem.at[h])
        for h in range(chunks)
    ]

    def project(h):
        if h == 0:
            basis_copy.wait()
        for f in flows:
            span = slice(f * per * BLK, (f + 1) * per * BLK)
            part = one[h].finish(f)
            pieces = []
            for i in range(per):
                blk = f * per + i
                pieces.append(part[i] * weight[blk : blk + 1, :])
            wide = jnp.concatenate(pieces, axis=1)
            dual[spans[h], span] = wide
            coeff = jnp.dot(wide.astype(BF16), basis[span], preferred_element_type=F32)
            if f == 0:
                cacc[h] = coeff
            else:
                cacc[h] += coeff
        sums[h].spread(cacc.at[h])

    def solve(h):
        if h == 0:
            coarse_copy.wait()
        sums[h].arrive()
        groups, width = call.shape[1], call.shape[3]
        solved = jnp.dot(call[h, 0], coarse[0:width], preferred_element_type=F32)
        for c in range(1, groups):
            solved = solved + jnp.dot(
                call[h, c], coarse[c * width : (c + 1) * width], preferred_element_type=F32
            )
        return solved.astype(BF16)

    def rise(h, solved, part_of):
        for f in part_of:
            span = slice(f * per * BLK, (f + 1) * per * BLK)
            part = lax.dot_general(
                solved, basis[span], (((1,), (1,)), ((), ())), preferred_element_type=F32
            )
            start_ref[spans[h], span] = part
            for i in range(per):
                where = me * own_blocks + f * per + i
                gat[h][where] = part[:, i * BLK : (i + 1) * BLK].astype(BF16)
            gathers[h].begin(f)

    def apply(h, lo, hi):
        def second(s, carry):
            picked = [gat[h][target_of(s * per_sub + j)] for j in range(per_sub)]
            held = jnp.concatenate(picked, axis=1)
            prod = jnp.dot(held, operators[s], preferred_element_type=F32)
            add_runs(s, spans[h], prod)
            return carry

        lax.fori_loop(lo, hi, second, 0)

    def conclude(h):
        for f in flows:
            part = two[h].finish(f)
            for i in range(per):
                blk = f * per + i
                span = slice(blk * BLK, (blk + 1) * BLK)
                resid_ref[spans[h], span] = (
                    dual[spans[h], span] - part[i] * weight[blk : blk + 1, :]
                )

    every = range(chunks)
    half = FLOWS // 2
    cut = [subs * i // 8 for i in CUTS]

    def wrap_up(h):
        one[h].drain()
        sums[h].drain()

    for h in every:
        one[h].step(0)
    if chunks == 1:
        for t in range(1, bits):
            one[0].step(t)
        project(0)
        sums[0].gather()
        rise(0, solve(0), flows)
        for u in range(1, bits):
            gathers[0].step(u)
        gathers[0].arrive()
        wrap_up(0)
        apply(0, 0, subs)
        for t in range(bits):
            two[0].step(t)
        conclude(0)
    else:
        for t in range(1, bits):
            one[0].step(t)
        one[1].step(1)
        project(0)
        for t in range(2, bits):
            one[1].step(t)
        sums[0].gather()
        project(1)
        x0 = solve(0)
        rise(0, x0, flows[:half])
        sums[1].gather()
        rise(0, x0, flows[half:])
        gathers[0].step(1)
        x1 = solve(1)
        rise(1, x1, flows[:half])
        gathers[0].step(2, flows[:half])
        rise(1, x1, flows[half:])
        gathers[0].step(2, flows[half:])
        wrap_up(0)
        gathers[0].arrive()
        apply(0, 0, cut[0])
        gathers[1].step(1)
        apply(0, cut[0], cut[1])
        gathers[1].step(2, flows[:half])
        apply(0, cut[1], subs)
        gathers[1].step(2, flows[half:])
        two[0].step(0)
        wrap_up(1)
        gathers[1].arrive()
        apply(1, 0, cut[2])
        two[0].step(1)
        apply(1, cut[2], subs)
        two[0].step(2)
        two[1].step(0)
        two[1].step(1)
        conclude(0)
        two[1].step(2)
        conclude(1)

    for h in range(chunks):
        gathers[h].drain()
        two[h].drain()


def hand_over(start_in, resid_in, start_out, resid_out, sem):
    copies = [
        pltpu.make_async_copy(start_in, start_out, sem.at[0]),
        pltpu.make_async_copy(resid_in, resid_out, sem.at[1]),
    ]
    for copy in copies:
        copy.start()
    for copy in copies:
        copy.wait()


def chunks_of(n, columns, dirs):
    half = columns // 2
    groups = n // min(n, max(1, half // 16))
    return 2 if half % 16 == 0 and dirs // groups >= LANES else 1


def per_device(n, loads, operators, owner, dual_block, scale_index, basis, coarse):
    subs, columns, rows_in = loads.shape
    local_rows = basis.shape[0]
    own_blocks = local_rows // BLK
    duals = n * own_blocks
    nblocks = owner.shape[0]
    spare = jnp.zeros((-2 * nblocks % LANES,), I32)
    meta = jnp.concatenate([owner.reshape(-1), dual_block, spare, scale_index])
    meta = meta.reshape(-1, LANES)
    per = own_blocks // FLOWS
    dirs = coarse.shape[0]
    chunks = chunks_of(n, columns, dirs)
    high = columns // chunks
    rows = min(n, high // 16)
    groups = n // rows
    entries = max(LANES, duals)
    vmem = pl.BlockSpec(memory_space=pltpu.VMEM)
    hbm = pl.BlockSpec(memory_space=pl.ANY)
    dma = pltpu.SemaphoreType.DMA
    out = jax.ShapeDtypeStruct((columns, local_rows), F32)
    blocks = pltpu.VMEM((chunks, FLOWS, n - 1, per, high, BLK), BF16)
    results = pl.pallas_call(
        functools.partial(kernel, n),
        out_shape=(out, out),
        in_specs=[vmem] + [hbm] * 4,
        out_specs=(vmem, vmem),
        scratch_shapes=[
            pltpu.VMEM(loads.shape, BF16),
            pltpu.VMEM(operators.shape, BF16),
            pltpu.VMEM(basis.shape, BF16),
            pltpu.VMEM(coarse.shape, BF16),
            pltpu.VMEM((nblocks + 1, columns, BLK), F32),
            pltpu.VMEM((8, entries), I32),
            pltpu.SMEM((8, entries), I32),
            blocks,
            blocks,
            pltpu.VMEM((chunks, high, dirs), F32),
            pltpu.VMEM((chunks, groups, high, dirs // groups), BF16),
            pltpu.VMEM((chunks, n, high // rows, dirs // groups), BF16),
            pltpu.VMEM((chunks, groups, high, dirs // groups), BF16),
            pltpu.VMEM((columns, local_rows), F32),
            dma((3,)),
            dma((subs,)),
            dma((subs,)),
            dma((chunks,)),
            dma((chunks, FLOWS, n // 2)),
            dma((chunks, 4)),
            dma((chunks,)),
            dma((chunks, FLOWS, n // 2)),
        ]
        + [pltpu.VMEM((duals, high, BLK), BF16)] * chunks,
        compiler_params=pltpu.CompilerParams(
            collective_id=0, has_side_effects=True, vmem_limit_bytes=VMEM_LIMIT
        ),
        name="feti",
    )(
        meta,
        loads,
        operators,
        basis,
        coarse,
    )
    return pl.pallas_call(
        hand_over,
        out_shape=(out, out),
        in_specs=[vmem, vmem],
        out_specs=(hbm, hbm),
        scratch_shapes=[dma((2,))],
        compiler_params=pltpu.CompilerParams(vmem_limit_bytes=4 * out.size * 4),
        name="hand_over",
    )(*results)


def solution(mesh):
    return jax.shard_map(
        functools.partial(per_device, mesh.shape["sub"]),
        mesh=mesh,
        in_specs=(
            P("sub", "rep", None),
            P("sub", None, None),
            P("sub", None),
            P("sub"),
            P("sub"),
            P("sub", None),
            P(),
        ),
        out_specs=(P("rep", "sub"), P("rep", "sub")),
        check_vma=False,
    )
```

```python
import functools

import jax
import jax.numpy as jnp
from jax import lax
from jax.experimental import pallas as pl
from jax.experimental.pallas import tpu as pltpu
from jax.sharding import PartitionSpec as P

BLK = 128
LANES = 128
FLOWS = 4
BY_FLOW = (0,)
CUTS = (2, 5, 2)
AHEAD = 4
MESH = pl.DeviceIdType.MESH
VMEM_LIMIT = 55 * 1000 * 1000
F32 = jnp.float32
BF16 = jnp.bfloat16
I32 = jnp.int32


def flip(me, r, bits):
    out = me
    for b in range(bits):
        if (r >> b) & 1:
            out = out + (1 - 2 * (me // (1 << b) % 2)) * (1 << b)
    return out


def plan(bits, flows):
    rest = list(range(1, bits))
    return [[0] + (rest if f % 2 == 0 else rest[::-1]) for f in range(flows)]


def step_of(r, order):
    for t, b in enumerate(order):
        if (r >> b) & 1:
            return t
    return len(order)


def slot_table(n, order):
    table, done = {}, 0
    for t, b in enumerate(order):
        done |= 1 << b
        for r in range(n):
            if r & done == 0:
                table[(t, r)] = len(table)
    return table


def remote(src, dst, send_sem, recv_sem, peer):
    return pltpu.make_async_remote_copy(
        src_ref=src,
        dst_ref=dst,
        send_sem=send_sem,
        recv_sem=recv_sem,
        device_id={"sub": peer},
        device_id_type=MESH,
    )


class ReduceScatter:
    def __init__(self, n, bits, me, local, stage, recv, send_sem, recv_sem):
        self.n, self.bits, self.me, self.local = n, bits, me, local
        self.stage, self.recv = stage, recv
        self.send_sem, self.recv_sem = send_sem, recv_sem
        self.orders = plan(bits, FLOWS)
        self.tables = [slot_table(n, order) for order in self.orders]
        self.met = [False] * FLOWS

    def sem_of(self, f, slot):
        return self.recv_sem.at[f, max(0, slot - self.n // 2 + 1)]

    def wait(self, f, r, t):
        slot = self.tables[f][(t, r)]
        where = self.recv.at[f, slot]
        if t == 0:
            if self.met[f]:
                return
            self.met[f] = True
            where = self.recv.at[f, pl.ds(0, self.n // 2)]
        peer = flip(self.me, 1 << self.orders[f][t], self.bits)
        remote(where, where, self.send_sem, self.sem_of(f, slot), peer).wait_recv()

    def total(self, f, r, steps):
        part = self.local(f, flip(self.me, r, self.bits))
        for t in range(steps):
            self.wait(f, r, t)
            part = part + self.recv[f, self.tables[f][(t, r)]].astype(F32)
        return part

    def step(self, t, flows=range(FLOWS)):
        group = []
        for f in flows:
            for r in range(self.n):
                if step_of(r, self.orders[f]) == t:
                    land = r ^ (1 << self.orders[f][t])
                    when = step_of(land, self.orders[f])
                    group.append((f if t in BY_FLOW else 0, when, f, r, land))
        for _, _, f, r, land in sorted(group):
            self.stage[f, r - 1] = self.total(f, r, t).astype(BF16)
            slot = self.tables[f][(t, land)]
            peer = flip(self.me, 1 << self.orders[f][t], self.bits)
            remote(
                self.stage.at[f, r - 1],
                self.recv.at[f, slot],
                self.send_sem,
                self.sem_of(f, slot),
                peer,
            ).start()

    def finish(self, f):
        return self.total(f, 0, self.bits)

    def drain(self):
        peer = flip(self.me, 1, self.bits)
        remote(self.stage, self.recv, self.send_sem, self.recv_sem.at[0, 0], peer).wait_send()


class SumToAll:
    def __init__(self, n, bits, me, part, got, every, sems):
        self.n, self.bits, self.me = n, bits, me
        self.part, self.got, self.every, self.sems = part, got, every, sems
        self.groups, self.wide = part.shape[0], part.shape[2]
        self.rows = n // self.groups
        self.tall = part.shape[1] // self.rows

    def piece(self, ref, p):
        start = pl.multiple_of(p % self.rows * self.tall, self.tall)
        return ref.at[p // self.rows, pl.ds(start, self.tall)]

    def whole(self, way):
        where = self.got.at[pl.ds(1, self.n - 1)]
        peer = flip(self.me, 1, self.bits)
        return remote(where, where, self.sems.at[2 * way], self.sems.at[2 * way + 1], peer)

    def spread(self, acc):
        for c in range(self.groups):
            self.part[c] = acc[:, c * self.wide : (c + 1) * self.wide].astype(BF16)
        for r in reversed(range(1, self.n)):
            peer = flip(self.me, r, self.bits)
            src, dst = self.piece(self.part, peer), self.got.at[r]
            remote(src, dst, self.sems.at[0], self.sems.at[1], peer).start()

    def gather(self):
        mine = self.piece(self.part, self.me)[...].astype(F32)
        self.whole(0).wait_recv()
        for r in range(1, self.n):
            mine = mine + self.got[r].astype(F32)
        where = self.piece(self.every, self.me)
        where[...] = mine.astype(BF16)
        for r in reversed(range(1, self.n)):
            peer = flip(self.me, r, self.bits)
            remote(where, where, self.sems.at[2], self.sems.at[3], peer).start()

    def arrive(self):
        self.whole(1).wait_recv()

    def drain(self):
        self.whole(0).wait_send()
        self.whole(1).wait_send()


class AllGather:
    def __init__(self, n, bits, me, own_blocks, store, send_sem, recv_sem):
        self.n, self.bits, self.me = n, bits, me
        self.own_blocks, self.per = own_blocks, own_blocks // FLOWS
        self.store, self.send_sem, self.recv_sem = store, send_sem, recv_sem
        self.orders = [order[::-1] for order in plan(bits, FLOWS)]
        self.known = [[0] for _ in range(FLOWS)]

    def copy_of(self, f, r, land, b):
        base = flip(self.me, r, self.bits) * self.own_blocks + f * self.per
        where = self.store.at[pl.ds(base, self.per)]
        sem = self.recv_sem.at[0, 0] if land % 2 else self.recv_sem.at[f, land // 2]
        return remote(where, where, self.send_sem, sem, flip(self.me, 1 << b, self.bits))

    def send(self, f, r, u):
        for b in self.orders[f][u:]:
            self.copy_of(f, r, r ^ (1 << b), b).start()

    def begin(self, f):
        self.send(f, 0, 0)

    def step(self, u, flows=range(FLOWS)):
        for f in flows:
            last = 1 << self.orders[f][u - 1]
            fresh = [r ^ last for r in self.known[f]]
            for r in fresh:
                self.copy_of(f, r, r, 1).wait_recv()
                self.send(f, r, u)
            self.known[f] = self.known[f] + fresh

    def whole(self, count):
        where = self.store.at[pl.ds(0, count * self.own_blocks)]
        peer = flip(self.me, 1, self.bits)
        return remote(where, where, self.send_sem, self.recv_sem.at[0, 0], peer)

    def arrive(self):
        self.whole(self.n // 2).wait_recv()

    def drain(self):
        self.whole(self.n - 1).wait_send()


def find_links(target, index, duals):
    nblocks = target.shape[1]
    rows = lax.broadcasted_iota(I32, (nblocks, nblocks), 0)
    cols = lax.broadcasted_iota(I32, (nblocks, nblocks), 1)
    wide = jnp.broadcast_to(target, (nblocks, nblocks))
    down = jnp.max(jnp.where(rows == cols, wide, -1), axis=1, keepdims=True)
    before = jnp.where((down == wide) & (rows < cols), rows, -1)
    before = jnp.max(before, axis=0, keepdims=True)
    names = lax.broadcasted_iota(I32, (nblocks, duals), 1)
    places = lax.broadcasted_iota(I32, (nblocks, duals), 0)
    last = jnp.max(jnp.where(down == names, places, -1), axis=0, keepdims=True)
    index[0:1, 0:nblocks] = target
    index[1:2, 0:nblocks] = jnp.where(before < 0, nblocks, before)
    index[2:3, 0:duals] = jnp.where(last < 0, nblocks, last)


def kernel(
    n,
    meta,
    loads_hbm,
    operators_hbm,
    basis_hbm,
    coarse_hbm,
    start_ref,
    resid_ref,
    loads,
    operators,
    basis,
    coarse,
    runs,
    index,
    table,
    stage,
    recv,
    cacc,
    cpart,
    cgot,
    call,
    dual,
    in_sem,
    op_sem,
    load_sem,
    send_sem,
    recv_sem,
    sum_sem,
    gsend_sem,
    grecv_sem,
    *gat,
):
    bits = n.bit_length() - 1
    me = lax.axis_index("sub")
    subs, columns, rows_in = loads.shape
    per_sub = rows_in // BLK
    nblocks = subs * per_sub
    chunks, (duals, high, _) = len(gat), gat[0].shape
    own_blocks = duals // n
    per = own_blocks // FLOWS
    flows = range(FLOWS)

    def target_of(i):
        return table[0, i]

    def before(i):
        return table[1, i]

    def last(i):
        return table[2, i]


    barrier = pltpu.get_barrier_semaphore()
    for r in range(1, n):
        pl.semaphore_signal(
            barrier, inc=1, device_id={"sub": flip(me, r, bits)}, device_id_type=MESH
        )
    basis_copy = pltpu.make_async_copy(basis_hbm, basis, in_sem.at[0])
    coarse_copy = pltpu.make_async_copy(coarse_hbm, coarse, in_sem.at[1])
    table_copy = pltpu.make_async_copy(index, table, in_sem.at[2])

    def load_copy(s):
        return pltpu.make_async_copy(loads_hbm.at[s], loads.at[s], load_sem.at[s])

    def op_copy(s):
        return pltpu.make_async_copy(operators_hbm.at[s], operators.at[s], op_sem.at[s])

    ahead = min(AHEAD, subs)
    for s in range(ahead):
        load_copy(s).start()
        op_copy(s).start()
    head = meta.shape[0] - own_blocks
    names = jnp.concatenate([meta[i : i + 1] for i in range(head)], axis=1)
    target = names[:, :nblocks] * own_blocks + names[:, nblocks : 2 * nblocks]
    find_links(target, index, duals)
    table_copy.start()
    runs[nblocks] = jnp.zeros((columns, BLK), F32)
    weight = 1.0 / (1.0 + meta[head:].astype(F32))
    table_copy.wait()

    def add_runs(s, span, prod):
        for j in range(per_sub):
            row = s * per_sub + j
            term = prod[:, j * BLK : (j + 1) * BLK].astype(BF16).astype(F32)
            runs[row, span] = term + runs[before(row), span]

    def first(s, carry):
        load_copy(s).wait()
        op_copy(s).wait()

        @pl.when(s + ahead < subs)
        def _():
            load_copy(s + ahead).start()
            op_copy(s + ahead).start()

        @pl.when(s + ahead == subs)
        def _():
            basis_copy.start()
            coarse_copy.start()

        add_runs(s, slice(None), jnp.dot(loads[s], operators[s], preferred_element_type=F32))
        return carry

    lax.fori_loop(0, subs, first, 0)
    pl.semaphore_wait(barrier, n - 1)

    spans = [slice(h * high, (h + 1) * high) for h in range(chunks)]

    def scatter_of(h):
        def local(f, owner):
            base = owner * own_blocks + f * per
            return jnp.stack([runs[last(base + i), spans[h]] for i in range(per)])

        return ReduceScatter(
            n, bits, me, local, stage.at[h], recv.at[h], send_sem.at[h], recv_sem.at[h]
        )

    one = [scatter_of(h) for h in range(chunks)]
    two = [scatter_of(h) for h in range(chunks)]
    sums = [
        SumToAll(
            n, bits, me, cpart.at[h], cgot.at[h], call.at[h], sum_sem.at[h]
        )
        for h in range(chunks)
    ]
    gathers = [
        AllGather(n, bits, me, own_blocks, gat[h], gsend_sem.at[h], grecv_sem.at[h])
        for h in range(chunks)
    ]

    def project(h):
        if h == 0:
            basis_copy.wait()
        for f in flows:
            span = slice(f * per * BLK, (f + 1) * per * BLK)
            part = one[h].finish(f)
            pieces = []
            for i in range(per):
                blk = f * per + i
                pieces.append(part[i] * weight[blk : blk + 1, :])
            wide = jnp.concatenate(pieces, axis=1)
            dual[spans[h], span] = wide
            coeff = jnp.dot(wide.astype(BF16), basis[span], preferred_element_type=F32)
            if f == 0:
                cacc[h] = coeff
            else:
                cacc[h] += coeff
        sums[h].spread(cacc.at[h])

    def solve(h):
        if h == 0:
            coarse_copy.wait()
        sums[h].arrive()
        groups, width = call.shape[1], call.shape[3]
        solved = jnp.dot(call[h, 0], coarse[0:width], preferred_element_type=F32)
        for c in range(1, groups):
            solved = solved + jnp.dot(
                call[h, c], coarse[c * width : (c + 1) * width], preferred_element_type=F32
            )
        return solved.astype(BF16)

    def rise(h, solved, part_of):
        for f in part_of:
            span = slice(f * per * BLK, (f + 1) * per * BLK)
            part = lax.dot_general(
                solved, basis[span], (((1,), (1,)), ((), ())), preferred_element_type=F32
            )
            start_ref[spans[h], span] = part
            for i in range(per):
                where = me * own_blocks + f * per + i
                gat[h][where] = part[:, i * BLK : (i + 1) * BLK].astype(BF16)
            gathers[h].begin(f)

    def apply(h, lo, hi):
        def second(s, carry):
            picked = [gat[h][target_of(s * per_sub + j)] for j in range(per_sub)]
            held = jnp.concatenate(picked, axis=1)
            prod = jnp.dot(held, operators[s], preferred_element_type=F32)
            add_runs(s, spans[h], prod)
            return carry

        lax.fori_loop(lo, hi, second, 0)

    def conclude(h):
        for f in flows:
            part = two[h].finish(f)
            for i in range(per):
                blk = f * per + i
                span = slice(blk * BLK, (blk + 1) * BLK)
                resid_ref[spans[h], span] = (
                    dual[spans[h], span] - part[i] * weight[blk : blk + 1, :]
                )

    every = range(chunks)
    half = FLOWS // 2
    cut = [subs * i // 8 for i in CUTS]

    def wrap_up(h):
        one[h].drain()
        sums[h].drain()

    for h in every:
        one[h].step(0)
    if chunks == 1:
        for t in range(1, bits):
            one[0].step(t)
        project(0)
        sums[0].gather()
        rise(0, solve(0), flows)
        for u in range(1, bits):
            gathers[0].step(u)
        gathers[0].arrive()
        wrap_up(0)
        apply(0, 0, subs)
        for t in range(bits):
            two[0].step(t)
        conclude(0)
    else:
        for t in range(1, bits):
            one[0].step(t)
        one[1].step(1)
        project(0)
        for t in range(2, bits):
            one[1].step(t)
        sums[0].gather()
        project(1)
        x0 = solve(0)
        rise(0, x0, flows[:half])
        sums[1].gather()
        rise(0, x0, flows[half:])
        gathers[0].step(1)
        x1 = solve(1)
        rise(1, x1, flows[:half])
        gathers[0].step(2, flows[:half])
        rise(1, x1, flows[half:])
        gathers[0].step(2, flows[half:])
        wrap_up(0)
        gathers[0].arrive()
        apply(0, 0, cut[0])
        gathers[1].step(1)
        apply(0, cut[0], cut[1])
        gathers[1].step(2, flows[:half])
        apply(0, cut[1], subs)
        gathers[1].step(2, flows[half:])
        two[0].step(0)
        wrap_up(1)
        gathers[1].arrive()
        apply(1, 0, cut[2])
        two[0].step(1)
        apply(1, cut[2], subs)
        two[0].step(2)
        two[1].step(0)
        two[1].step(1)
        conclude(0)
        two[1].step(2)
        conclude(1)

    for h in range(chunks):
        gathers[h].drain()
        two[h].drain()


def hand_over(start_in, resid_in, start_out, resid_out, sem):
    copies = [
        pltpu.make_async_copy(start_in, start_out, sem.at[0]),
        pltpu.make_async_copy(resid_in, resid_out, sem.at[1]),
    ]
    for copy in copies:
        copy.start()
    for copy in copies:
        copy.wait()


def chunks_of(n, columns, dirs):
    half = columns // 2
    groups = n // min(n, max(1, half // 16))
    return 2 if half % 16 == 0 and dirs // groups >= LANES else 1


def per_device(n, loads, operators, owner, dual_block, scale_index, basis, coarse):
    subs, columns, rows_in = loads.shape
    local_rows = basis.shape[0]
    own_blocks = local_rows // BLK
    duals = n * own_blocks
    nblocks = owner.shape[0]
    spare = jnp.zeros((-2 * nblocks % LANES,), I32)
    meta = jnp.concatenate([owner.reshape(-1), dual_block, spare, scale_index])
    meta = meta.reshape(-1, LANES)
    per = own_blocks // FLOWS
    dirs = coarse.shape[0]
    chunks = chunks_of(n, columns, dirs)
    high = columns // chunks
    rows = min(n, high // 16)
    groups = n // rows
    entries = max(LANES, duals)
    vmem = pl.BlockSpec(memory_space=pltpu.VMEM)
    hbm = pl.BlockSpec(memory_space=pl.ANY)
    dma = pltpu.SemaphoreType.DMA
    out = jax.ShapeDtypeStruct((columns, local_rows), F32)
    blocks = pltpu.VMEM((chunks, FLOWS, n - 1, per, high, BLK), BF16)
    results = pl.pallas_call(
        functools.partial(kernel, n),
        out_shape=(out, out),
        in_specs=[vmem] + [hbm] * 4,
        out_specs=(vmem, vmem),
        scratch_shapes=[
            pltpu.VMEM(loads.shape, BF16),
            pltpu.VMEM(operators.shape, BF16),
            pltpu.VMEM(basis.shape, BF16),
            pltpu.VMEM(coarse.shape, BF16),
            pltpu.VMEM((nblocks + 1, columns, BLK), F32),
            pltpu.VMEM((8, entries), I32),
            pltpu.SMEM((8, entries), I32),
            blocks,
            blocks,
            pltpu.VMEM((chunks, high, dirs), F32),
            pltpu.VMEM((chunks, groups, high, dirs // groups), BF16),
            pltpu.VMEM((chunks, n, high // rows, dirs // groups), BF16),
            pltpu.VMEM((chunks, groups, high, dirs // groups), BF16),
            pltpu.VMEM((columns, local_rows), F32),
            dma((3,)),
            dma((subs,)),
            dma((subs,)),
            dma((chunks,)),
            dma((chunks, FLOWS, n // 2)),
            dma((chunks, 4)),
            dma((chunks,)),
            dma((chunks, FLOWS, n // 2)),
        ]
        + [pltpu.VMEM((duals, high, BLK), BF16)] * chunks,
        compiler_params=pltpu.CompilerParams(
            collective_id=0, has_side_effects=True, vmem_limit_bytes=VMEM_LIMIT
        ),
        name="feti",
    )(
        meta,
        loads,
        operators,
        basis,
        coarse,
    )
    return pl.pallas_call(
        hand_over,
        out_shape=(out, out),
        in_specs=[vmem, vmem],
        out_specs=(hbm, hbm),
        scratch_shapes=[dma((2,))],
        compiler_params=pltpu.CompilerParams(vmem_limit_bytes=4 * out.size * 4),
        name="hand_over",
    )(*results)


def solution(mesh):
    return jax.shard_map(
        functools.partial(per_device, mesh.shape["sub"]),
        mesh=mesh,
        in_specs=(
            P("sub", "rep", None),
            P("sub", None, None),
            P("sub", None),
            P("sub"),
            P("sub"),
            P("sub", None),
            P(),
        ),
        out_specs=(P("rep", "sub"), P("rep", "sub")),
        check_vma=False,
    )
```
